32 devices in a mesh: dap: 8 (over z, core), ch: 4 (over y, x).
Axes of the slice: x: 2, y: 2, z: 4, core: 2. Of those that a mesh axis runs over, the one named last changes fastest.
Arguments:
- pair_rep: bfloat16 [120, 120, 128], P('dap', 'ch'), may hold values from -400 to 400
- residue_mask: int32 [120], replicated, may hold values 0 or 1
- w_proj: bfloat16 [128, 512], replicated, may hold values from -0.5 to 0.5
- w_gate: bfloat16 [128, 128], replicated, may hold values from -0.5 to 0.5
- w_out: bfloat16 [128, 128], replicated, may hold values from -0.5 to 0.5
- cotangent: bfloat16 [120, 120, 128], P('dap', 'ch'), may hold values from -6 to 6
Outputs:
- pair_update: bfloat16 [120, 120, 128], P('dap', 'ch')
- grad_pair: bfloat16 [120, 120, 128], P('dap', 'ch')
The draws below stay inside these ranges and needn't reach their ends.
Inputs may be any that keep to these rules, and one draw needn't show every extreme that they name: `residue_mask`: 1 marks a residue of the crop, 0 a padding position.
All inputs are finite; a program needn't handle non-finite values.
Results may differ from the reference program's by a relative error of at most 0.0085.
Values may be sent and summed in bfloat16 or wider, within the bound.
No kernel may reach another device: no remote copies, remote signals or barrier semaphores. Data moves between devices by JAX's collectives and lax.ppermute only.
A program may use at most 64 MiB of HBM per device.

```python
import math
import jax
import jax.numpy as jnp
from jax import lax

C = 128
H = 128
N_RES = 120


def draw_pair_rep(key, part):
    subkeys = jax.random.split(jax.random.fold_in(key, 11), 4)
    full_shape = (N_RES, N_RES, C)
    channel_scale = jnp.exp(jax.random.uniform(subkeys[2], (1, 1, C), jnp.float32, 0.0, math.log(4.0)))
    cell_offset = 0.5 * jnp.clip(jax.random.normal(subkeys[3], (N_RES, N_RES, 1), jnp.float32), -4.0, 4.0)
    cell_scale = jnp.exp(jax.random.uniform(subkeys[1], (N_RES, N_RES, 1), jnp.float32, 0.0, math.log(10.0)))
    base_values = jnp.clip(jax.random.normal(subkeys[0], full_shape, jnp.float32), -4.0, 4.0) + cell_offset
    return (base_values * cell_scale * channel_scale).astype(jnp.bfloat16)


def touch_ends(result, key, least, largest):
    longest = result.shape.index(max(result.shape))
    spots = []
    for shift in (0, 1):
        where = [jax.random.randint(jax.random.fold_in(key, axis), (), 0, length) for axis, length in enumerate(result.shape)]
        where[longest] = (where[longest] + shift) % result.shape[longest]
        spots.append(tuple(where))
    return result.at[spots[0]].set(least).at[spots[1]].set(largest)


def level_of(key, extent, shards, least, largest):
    factor_of = 1.0
    for position, shards_of in shards:
        draws = jax.random.uniform(jax.random.fold_in(jax.random.fold_in(key, 6), position), (shards_of,), jnp.float32, least / len(shards), largest / len(shards))
        factor_of = factor_of * jnp.repeat(jnp.exp(draws), extent[position] // shards_of).reshape((-1,) + (1,) * (len(extent) - 1 - position))
    return factor_of


def normal_values(rng, shape, scale, bound, cuts=(), dtype=jnp.bfloat16):
    factor_of = level_of(rng, shape, cuts, -0.22, 0.18) if cuts else 1.0
    values = jax.random.normal(rng, shape, jnp.float32) * scale * factor_of
    return jnp.minimum(jnp.maximum(values, -bound), bound).astype(dtype)


def setup_inputs(seed: int = 0) -> dict:
    key_list = jax.random.split(jax.random.key(seed), 7)
    pair_rep = draw_pair_rep(jax.random.fold_in(key_list[6], 71), 0)
    residue_mask = touch_ends((jax.random.randint(key_list[1], (N_RES,), 0, 8) < 7).astype(jnp.int32), jax.random.fold_in(key_list[1], 1), 0, 1)
    w_proj = normal_values(key_list[2], (C, 4 * H), C ** -0.5, 0.5)
    w_gate = normal_values(key_list[3], (C, C), C ** -0.5, 0.5)
    w_out = normal_values(key_list[4], (H, C), H ** -0.5, 0.5)
    cotangent = normal_values(key_list[5], (N_RES, N_RES, C), 1.0, 6.0, ((0, 8), (1, 4)))
    return dict(pair_rep=pair_rep, residue_mask=residue_mask, w_proj=w_proj, w_gate=w_gate, w_out=w_out, cotangent=cotangent)


EPSILON = 1e-05

def normalize(values, axis):
    center = lax.optimization_barrier(jnp.mean(values, axis=axis, keepdims=True))
    spread = values - center
    scale_inv = lax.rsqrt(lax.optimization_barrier(jnp.mean(spread * spread, axis=axis, keepdims=True)) + EPSILON)
    return (spread * scale_inv, scale_inv)

def norm_back(grad_in, normed, scale_inv, axis):
    first = lax.optimization_barrier(jnp.mean(grad_in, axis=axis, keepdims=True))
    second = lax.optimization_barrier(jnp.mean(grad_in * normed, axis=axis, keepdims=True))
    return scale_inv * (grad_in - first - normed * second)

def reference(pair_rep, residue_mask, w_proj, w_gate, w_out, cotangent):
    live_flags = residue_mask.astype(jnp.float32)
    pair_mask = (live_flags[:, None] * live_flags[None, :])[:, :, None]
    normed, pair_scale = normalize(pair_rep.astype(jnp.float32), 2)
    normed_half = normed.astype(jnp.bfloat16)
    flat_cells = normed_half.reshape(N_RES * N_RES, C)
    projected = jnp.dot(flat_cells, w_proj, preferred_element_type=jnp.float32).reshape(N_RES, N_RES, 4 * H)
    left_sig = jax.nn.sigmoid(projected[:, :, :H])
    left_val = projected[:, :, H:2 * H]
    right_sig = jax.nn.sigmoid(projected[:, :, 2 * H:3 * H])
    right_val = projected[:, :, 3 * H:]
    left_edges = (left_sig * left_val * pair_mask).astype(jnp.bfloat16)
    right_edges = (right_sig * right_val * pair_mask).astype(jnp.bfloat16)
    gate_values = jax.nn.sigmoid(jnp.dot(flat_cells, w_gate, preferred_element_type=jnp.float32).reshape(N_RES, N_RES, C))
    product = jnp.einsum('ikc,jkc->ijc', left_edges.astype(jnp.float32), right_edges.astype(jnp.float32)).astype(jnp.bfloat16)
    hidden_norm, hidden_scale = normalize(product.astype(jnp.float32), 2)
    hidden_half = hidden_norm.astype(jnp.bfloat16)
    projected_out = jnp.dot(hidden_half.reshape(N_RES * N_RES, H), w_out, preferred_element_type=jnp.float32).reshape(N_RES, N_RES, C)
    pair_update = (gate_values * projected_out).astype(jnp.bfloat16)
    upstream = cotangent.astype(jnp.float32)
    grad_out = (upstream * gate_values).astype(jnp.bfloat16)
    grad_logit = (upstream * projected_out * gate_values * (1.0 - gate_values)).astype(jnp.bfloat16)
    grad_hidden = jnp.dot(grad_out.reshape(N_RES * N_RES, C), w_out.T, preferred_element_type=jnp.float32).reshape(N_RES, N_RES, H)
    grad_product = norm_back(grad_hidden, hidden_norm, hidden_scale, 2).astype(jnp.bfloat16)
    grad_left = jnp.einsum('ijc,jkc->ikc', grad_product.astype(jnp.float32), right_edges.astype(jnp.float32)).astype(jnp.bfloat16)
    grad_right = jnp.einsum('ijc,ikc->jkc', grad_product.astype(jnp.float32), left_edges.astype(jnp.float32)).astype(jnp.bfloat16)
    masked_left = grad_left.astype(jnp.float32) * pair_mask
    masked_right = grad_right.astype(jnp.float32) * pair_mask
    grad_proj = jnp.concatenate([masked_left * left_val * left_sig * (1.0 - left_sig), masked_left * left_sig, masked_right * right_val * right_sig * (1.0 - right_sig), masked_right * right_sig], axis=2).astype(jnp.bfloat16)
    grad_normed = jnp.dot(grad_proj.reshape(N_RES * N_RES, 4 * H), w_proj.T, preferred_element_type=jnp.float32)
    grad_normed = grad_normed + jnp.dot(grad_logit.reshape(N_RES * N_RES, C), w_gate.T, preferred_element_type=jnp.float32)
    grad_pair = norm_back(grad_normed.reshape(N_RES, N_RES, C), normed, pair_scale, 2).astype(jnp.bfloat16)
    return (pair_update, grad_pair)
```

```python
import functools

import jax
import jax.numpy as jnp
from jax import lax
from jax.experimental import pallas as pl
from jax.experimental.pallas import tpu as pltpu
from jax.sharding import PartitionSpec as P

EPSILON = 1e-05
F32 = jnp.float32
BF16 = jnp.bfloat16
EARLY = 2
JB = 5


def pad_to(count, tile):
    return (count + tile - 1) // tile * tile


def normalize(values):
    center = jnp.mean(values, axis=-1, keepdims=True)
    spread = values - center
    scale = lax.rsqrt(jnp.mean(spread * spread, axis=-1, keepdims=True) + EPSILON)
    return spread * scale, scale


def norm_back(grad, normed, scale):
    first = jnp.mean(grad, axis=-1, keepdims=True)
    second = jnp.mean(grad * normed, axis=-1, keepdims=True)
    return scale * (grad - first - normed * second)


def matmul(a, b):
    return lax.dot_general(a, b, (((1,), (0,)), ((), ())), preferred_element_type=F32)


def matmul_t(a, b):
    return lax.dot_general(a, b, (((1,), (1,)), ((), ())), preferred_element_type=F32)


def col_mask(mask_ref, start, count, pitch, channels):
    row = lax.broadcasted_iota(jnp.int32, (pitch, channels), 0)
    flags = jnp.zeros((pitch, channels), F32)
    for k in range(count):
        flags = jnp.where(row == k, mask_ref[start + k].astype(F32), flags)
    return flags


def load_cells(cells_ref, scratch, first):
    rows, cols, channels = cells_ref.shape
    pitch = pad_to(cols, 16)
    for i in range(rows):
        at = (first + i) * pitch
        scratch[at : at + cols, :] = cells_ref[i].astype(F32)
        if pitch > cols:
            scratch[at + cols : at + pitch, :] = jnp.zeros((pitch - cols, channels), F32)


def row_of(ref, row):
    return ref[pl.ds(row, 8, stride=0), :]


def tiles(value):
    return value.reshape(value.shape[0] // 8, 8, value.shape[1])


def right_kernel(mask_ref, x_ref, w_ref, out_ref, xs):
    rows, cols, channels = x_ref.shape
    pitch = pad_to(cols, 16)
    hidden = w_ref.shape[1] // 2
    load_cells(x_ref, xs, 0)
    normed, _ = normalize(xs[...])
    projected = matmul(normed.astype(BF16), w_ref[...])
    right = jax.nn.sigmoid(projected[:, :hidden]) * projected[:, hidden:]
    flags = col_mask(mask_ref, lax.axis_index("ch") * cols, cols, pitch, hidden)
    start = lax.axis_index("dap") * rows
    for i in range(rows):
        block = slice(i * pitch, (i + 1) * pitch)
        live = flags * mask_ref[start + i].astype(F32)
        out_ref[block, :] = (right[block] * live).astype(BF16)


def left_kernel(mask_ref, x_ref, xp_ref, cot_ref, cotp_ref, w_ref, wg_ref,
                l_ref, lt_ref, gate_ref, cotm_ref, xs, ls, gs):
    rows, cols, channels = x_ref.shape
    pitch = pad_to(cols, 16)
    half = pad_to(rows, 16)
    hidden = w_ref.shape[1] // 2
    dap = lax.axis_index("dap")
    core = lax.rem(dap, 2)
    load_cells(x_ref, xs, 0)
    load_cells(xp_ref, xs, rows)
    normed, _ = normalize(xs[...])
    normed_half = normed.astype(BF16)
    projected = matmul(normed_half, w_ref[...])
    left = jax.nn.sigmoid(projected[:, :hidden]) * projected[:, hidden:]
    flags = col_mask(mask_ref, lax.axis_index("ch") * cols, cols, pitch, hidden)
    for i in range(2 * rows):
        owner = dap if i < rows else dap + 1 - 2 * core
        block = slice(i * pitch, (i + 1) * pitch)
        live = flags * mask_ref[owner * rows + i % rows].astype(F32)
        value = (left[block] * live).astype(BF16).astype(F32)
        l_ref[block, :] = value
        ls[block, :] = value
    tall = pad_to(2 * rows, 16)
    ls[2 * rows * pitch :, :] = jnp.zeros(((tall - 2 * rows) * pitch, hidden), F32)
    for k in range(cols):
        lt_ref[k * tall : (k + 1) * tall, :] = ls[pl.ds(k, tall, stride=pitch), :]
    gs[...] = jax.nn.sigmoid(matmul(normed_half, wg_ref[...]))

    def pick(out_ref):
        for i in range(2 * rows):
            low = gs[i * pitch : i * pitch + rows, :]
            high = gs[i * pitch + rows : i * pitch + 2 * rows, :]
            out_ref[i * half : i * half + rows, :] = jnp.where(core == 0, low, high)
            if half > rows:
                out_ref[i * half + rows : (i + 1) * half, :] = jnp.zeros((half - rows, channels), F32)

    pick(gate_ref)
    load_cells(cot_ref, gs, 0)
    load_cells(cotp_ref, gs, rows)
    pick(cotm_ref)


def factor_kernel(mask_ref, x_ref, w_ref, normed_ref, scale_ref, l1_ref, l2_ref, r1_ref, r2_ref, xs):
    rows, cols, channels = x_ref.shape
    pitch = pad_to(cols, 16)
    hidden = w_ref.shape[1] // 4
    load_cells(x_ref, xs, 0)
    normed, scale = normalize(xs[...])
    normed_ref[...] = normed
    scale_ref[...] = jnp.broadcast_to(scale, normed.shape)
    projected = matmul(normed.astype(BF16), w_ref[...])
    left_sig = jax.nn.sigmoid(projected[:, :hidden])
    right_sig = jax.nn.sigmoid(projected[:, 2 * hidden : 3 * hidden])
    left_in = projected[:, hidden : 2 * hidden] * left_sig * (1.0 - left_sig)
    right_in = projected[:, 3 * hidden :] * right_sig * (1.0 - right_sig)
    flags = col_mask(mask_ref, lax.axis_index("ch") * cols, cols, pitch, hidden)
    start = lax.axis_index("dap") * rows
    for i in range(rows):
        block = slice(i * pitch, (i + 1) * pitch)
        live = flags * mask_ref[start + i].astype(F32)
        l1_ref[block, :] = left_in[block] * live
        l2_ref[block, :] = left_sig[block] * live
        r1_ref[block, :] = right_in[block] * live
        r2_ref[block, :] = right_sig[block] * live


def product_part(lt_ref, r_ref, rs, out, rows, cols):
    pitch, half, tall = pad_to(cols, 16), pad_to(rows, 16), pad_to(2 * rows, 16)
    rs[...] = r_ref[...].astype(F32)

    def step(b, _):
        sums = [jnp.zeros((tall // 8, 8, rs.shape[1]), F32) for _ in range(JB)]
        for k in range(cols):
            left = tiles(lt_ref[k * tall : (k + 1) * tall, :])
            for n in range(JB):
                sums[n] = sums[n] + left * row_of(rs, (b * JB + n) * pitch + k)[None]
        for n in range(JB):
            out[pl.ds(b * JB + n, tall, stride=half), :] = sums[n].reshape(tall, rs.shape[1])
        return 0

    lax.fori_loop(0, rows // JB, step, 0)


def early_kernel(rows, cols, count, *refs):
    lt_ref, shards = refs[0], refs[1 : 1 + count]
    out_ref, rs = refs[1 + count :]
    for s in range(count):
        product_part(lt_ref, shards[s], rs, out_ref.at[s], rows, cols)


def late_kernel(rows, cols, blocks, early, *refs):
    lt_ref, early_ref = refs[:2]
    shards = refs[2 : 2 + blocks - early]
    outs = refs[2 + blocks - early : 2 + 2 * blocks - early]
    rs, ps = refs[2 + 2 * blocks - early :]
    chip, column = lax.axis_index("dap") // 2, lax.axis_index("ch")
    used = 2 * rows * pad_to(rows, 16)
    for s in range(early):
        ps[chip ^ s] = early_ref[s]
    for s in range(early, blocks):
        product_part(lt_ref, shards[s - early], rs, ps.at[chip ^ s], rows, cols)
    for t in range(blocks):
        outs[t][...] = ps[column ^ t, :used, :].astype(outs[t].dtype)


def middle_kernel(blocks, *refs):
    parts = refs[:blocks]
    gate_ref, cot_ref, w_ref, upd_ref, back_ref, logit_ref, gp_ref = refs[blocks:]
    total = parts[0][...]
    for t in range(1, blocks):
        total = total + parts[t][...].astype(F32)
    product = total.astype(BF16).astype(F32)
    hidden_norm, hidden_scale = normalize(product)
    out = matmul(hidden_norm.astype(BF16), w_ref[...])
    gate, upstream = gate_ref[...], cot_ref[...]
    grad_out = (upstream * gate).astype(BF16)
    grad_hidden = matmul_t(grad_out, w_ref[...])
    gp_ref[...] = norm_back(grad_hidden, hidden_norm, hidden_scale).astype(BF16)
    update = (gate * out).astype(BF16)
    logit = (upstream * out * gate * (1.0 - gate)).astype(BF16)
    own = upd_ref.shape[0]
    upd_ref[...] = update[:own]
    logit_ref[...] = logit[:own]
    back_ref[:own, :] = update[own:]
    back_ref[own:, :] = logit[own:]


def grad_right_part(l_ref, gs, block, store, rows, cols):
    pitch, half = pad_to(cols, 16), pad_to(rows, 16)
    piece = gs.at[block]

    def step(b, _):
        sums = [jnp.zeros((pitch // 8, 8, gs.shape[2]), F32) for _ in range(JB)]
        for i in range(2 * rows):
            left = tiles(l_ref[i * pitch : (i + 1) * pitch, :])
            for n in range(JB):
                sums[n] = sums[n] + left * row_of(piece, i * half + b * JB + n)[None]
        for n in range(JB):
            at = pl.multiple_of((b * JB + n) * pitch, pitch)
            store(pl.ds(at, pitch), sums[n].reshape(pitch, gs.shape[2]))
        return 0

    lax.fori_loop(0, rows // JB, step, 0)


def stage_pieces(pieces, gs):
    column = lax.axis_index("ch")
    for t, piece in enumerate(pieces):
        gs[column ^ t] = piece[...].astype(F32)


def send_right_kernel(rows, cols, blocks, *refs):
    l_ref, pieces = refs[0], refs[1 : 1 + blocks]
    outs, gs = refs[1 + blocks : 2 * blocks], refs[2 * blocks]
    chip = lax.axis_index("dap") // 2
    stage_pieces(pieces, gs)
    for s in range(1, blocks):
        def store(where, value, s=s):
            outs[s - 1][where, :] = value.astype(BF16)
        grad_right_part(l_ref, gs, chip ^ s, store, rows, cols)


def grad_left_kernel(rows, cols, blocks, *refs):
    l_ref, pieces, shards = refs[0], refs[1 : 1 + blocks], refs[1 + blocks : 1 + 2 * blocks]
    own_ref, send_ref, right_ref, gs, rs = refs[1 + 2 * blocks :]
    pitch, half = pad_to(cols, 16), pad_to(rows, 16)
    chip = lax.axis_index("dap") // 2
    stage_pieces(pieces, gs)
    for s in range(blocks):
        rs[chip ^ s] = shards[s][...].astype(F32)

    def left_rows(first, ref):
        def step(b, _):
            def block_step(m, sums):
                piece, shard = gs.at[m], rs.at[m]
                sums = list(sums)
                for j in range(rows):
                    right = tiles(shard[j * pitch : (j + 1) * pitch, :])
                    for n in range(JB):
                        row = (first + b * JB + n) * half + j
                        sums[n] = sums[n] + right * row_of(piece, row)[None]
                return tuple(sums)

            zero = jnp.zeros((pitch // 8, 8, gs.shape[2]), F32)
            sums = lax.fori_loop(0, blocks, block_step, (zero,) * JB)
            for n in range(JB):
                at = pl.multiple_of((b * JB + n) * pitch, pitch)
                ref[pl.ds(at, pitch), :] = sums[n].reshape(pitch, gs.shape[2]).astype(ref.dtype)
            return 0

        lax.fori_loop(0, rows // JB, step, 0)

    left_rows(rows, send_ref)
    left_rows(0, own_ref)

    def store(where, value):
        right_ref[where, :] = value

    grad_right_part(l_ref, gs, chip, store, rows, cols)


def finish_left_kernel(own_ref, got_ref, l1_ref, l2_ref, w_ref, wg_ref, upd_ref, logit_ref, back_ref,
                       out_ref, acc_ref, us, gs):
    rows, cols, channels = out_ref.shape
    pitch, half = pad_to(cols, 16), pad_to(rows, 16)
    mine = lax.rem(lax.axis_index("dap"), 2) == 0
    for i in range(rows):
        for scratch, ref, base in ((us, upd_ref, 0), (gs, logit_ref, rows * half)):
            here = ref[i * half : (i + 1) * half, :].astype(F32)[:rows]
            there = back_ref[base + i * half : base + (i + 1) * half, :].astype(F32)[:rows]
            scratch[i * pitch : i * pitch + rows, :] = jnp.where(mine, here, there)
            scratch[i * pitch + rows : i * pitch + 2 * rows, :] = jnp.where(mine, there, here)
            if pitch > cols:
                scratch[i * pitch + cols : (i + 1) * pitch, :] = jnp.zeros((pitch - cols, channels), F32)
        out_ref[i] = us[i * pitch : i * pitch + cols, :].astype(BF16)
    grad_left = (own_ref[...] + got_ref[...].astype(F32)).astype(BF16).astype(F32)
    hidden = own_ref.shape[1]
    acc = matmul_t((grad_left * l1_ref[...]).astype(BF16), w_ref[:, :hidden])
    acc = acc + matmul_t((grad_left * l2_ref[...]).astype(BF16), w_ref[:, hidden:])
    acc_ref[...] = acc + matmul_t(gs[...].astype(BF16), wg_ref[...])


def finish_kernel(blocks, *refs):
    parts = refs[:blocks]
    r1_ref, r2_ref, w_ref, acc_ref, normed_ref, scale_ref, out_ref = refs[blocks:]
    rows, cols, _ = out_ref.shape
    pitch = pad_to(cols, 16)
    total = parts[0][...]
    for s in range(1, blocks):
        total = total + parts[s][...].astype(F32)
    grad_right = total.astype(BF16).astype(F32)
    hidden = total.shape[1]
    grad = acc_ref[...] + matmul_t((grad_right * r1_ref[...]).astype(BF16), w_ref[:, :hidden])
    grad = grad + matmul_t((grad_right * r2_ref[...]).astype(BF16), w_ref[:, hidden:])
    result = norm_back(grad, normed_ref[...], scale_ref[...]).astype(BF16)
    for i in range(rows):
        out_ref[i] = result[i * pitch : i * pitch + cols]


VMEM = pl.BlockSpec(memory_space=pltpu.VMEM)
SMEM = pl.BlockSpec(memory_space=pltpu.SMEM)


def call(body, name, outs, args, scratch=(), smem=0, flops=10**7):
    outs = [jax.ShapeDtypeStruct(shape, dtype) for shape, dtype in outs]
    moved = sum(a.size * a.dtype.itemsize for a in list(args) + outs)
    return pl.pallas_call(
        body,
        name=name,
        out_shape=outs,
        in_specs=[SMEM] * smem + [VMEM] * (len(args) - smem),
        out_specs=[VMEM] * len(outs),
        scratch_shapes=[pltpu.VMEM(shape, F32) for shape in scratch],
        compiler_params=pltpu.CompilerParams(vmem_limit_bytes=60 << 20),
        cost_estimate=pl.CostEstimate(flops=flops, bytes_accessed=moved, transcendentals=0),
    )(*args)


def on_device(devices, blocks, x, mask, w_proj, w_gate, w_out, cot):
    rows, cols, channels = x.shape
    hidden = w_out.shape[0]
    pitch, half, tall = pad_to(cols, 16), pad_to(rows, 16), pad_to(2 * rows, 16)
    cells, wide, mids = rows * pitch, 2 * rows * pitch, 2 * rows * half
    if devices != 2 * blocks or cols != 2 * rows or blocks & (blocks - 1) or rows % JB:
        raise ValueError("unsupported split")
    w_left, w_right = w_proj[:, : 2 * hidden], w_proj[:, 2 * hidden :]

    def along_dap(value, s):
        return lax.ppermute(value, "dap", [(d, d ^ (2 * s)) for d in range(devices)])

    def along_ch(value, t):
        return lax.ppermute(value, "ch", [(h, h ^ t) for h in range(blocks)])

    def to_partner(value):
        return lax.ppermute(value, "dap", [(d, d ^ 1) for d in range(devices)])

    (right,) = call(right_kernel, "right", [((cells, hidden), BF16)], (mask, x, w_right),
                    [(cells, channels)], smem=1)
    shards = [right] + [along_dap(right, s) for s in range(1, blocks)]
    x_late, cot_late, _ = lax.optimization_barrier((x, cot, right))
    x_pair, cot_pair = to_partner(x_late), to_partner(cot_late)
    left, left_t, gate, upstream = call(
        left_kernel, "left",
        [((wide, hidden), F32), ((cols * tall, hidden), F32), ((mids, channels), F32), ((mids, channels), F32)],
        (mask, x_late, x_pair, cot_late, cot_pair, w_left, w_gate),
        [(wide, channels), (tall * pitch, hidden), (wide, channels)], smem=1)
    normed, scale, l1, l2, r1, r2 = call(
        factor_kernel, "factor", [((cells, hidden), F32)] * 6, (mask, x_late, w_proj),
        [(cells, channels)], smem=1)
    early = min(EARLY, blocks)
    (started,) = call(functools.partial(early_kernel, rows, cols, early), "early",
                      [((early, tall * half, hidden), F32)], (left_t, *shards[:early]), [(cells, hidden)])
    parts = call(functools.partial(late_kernel, rows, cols, blocks, early), "late",
                 [((mids, hidden), F32)] + [((mids, hidden), BF16)] * (blocks - 1),
                 (left_t, started, *shards[early:]),
                 [(cells, hidden), (blocks, tall * half, hidden)])
    parts = [parts[0]] + [along_ch(parts[t], t) for t in range(1, blocks)]
    update, back, logit, grad_product = call(
        functools.partial(middle_kernel, blocks), "middle",
        [((mids // 2, channels), BF16), ((mids, channels), BF16), ((mids // 2, channels), BF16), ((mids, hidden), BF16)],
        (*parts, gate, upstream, w_out))
    pieces = [grad_product] + [along_ch(grad_product, t) for t in range(1, blocks)]
    back = to_partner(back)
    sends = call(functools.partial(send_right_kernel, rows, cols, blocks), "send_right",
                 [((cells, hidden), BF16)] * (blocks - 1), (left, *pieces), [(blocks, mids, hidden)])
    gots = [along_dap(sends[s - 1], s) for s in range(1, blocks)]
    left_own, left_send, right_own = call(
        functools.partial(grad_left_kernel, rows, cols, blocks), "grad_left",
        [((cells, hidden), F32), ((cells, hidden), BF16), ((cells, hidden), F32)],
        (left, *pieces, *shards), [(blocks, mids, hidden), (blocks, cells, hidden)])
    left_got = to_partner(left_send)
    pair_update, acc = call(
        finish_left_kernel, "finish_left", [((rows, cols, channels), BF16), ((cells, channels), F32)],
        (left_own, left_got, l1, l2, w_left, w_gate, update, logit, back),
        [(cells, channels), (cells, channels)])
    (grad_pair,) = call(functools.partial(finish_kernel, blocks), "finish", [((rows, cols, channels), BF16)],
                        (right_own, *gots, r1, r2, w_right, acc, normed, scale))
    return pair_update, grad_pair


def solution(mesh):
    return jax.shard_map(
        functools.partial(on_device, mesh.shape["dap"], mesh.shape["ch"]),
        mesh=mesh,
        in_specs=(P("dap", "ch", None), P(), P(), P(), P(), P("dap", "ch", None)),
        out_specs=(P("dap", "ch", None), P("dap", "ch", None)),
        check_vma=False,
    )
```

```python
import functools

import jax
import jax.numpy as jnp
from jax import lax
from jax.experimental import pallas as pl
from jax.experimental.pallas import tpu as pltpu
from jax.sharding import PartitionSpec as P

EPSILON = 1e-05
F32 = jnp.float32
BF16 = jnp.bfloat16
EARLY = 2
JB = 5


def pad_to(count, tile):
    return (count + tile - 1) // tile * tile


def normalize(values):
    center = jnp.mean(values, axis=-1, keepdims=True)
    spread = values - center
    scale = lax.rsqrt(jnp.mean(spread * spread, axis=-1, keepdims=True) + EPSILON)
    return spread * scale, scale


def norm_back(grad, normed, scale):
    first = jnp.mean(grad, axis=-1, keepdims=True)
    second = jnp.mean(grad * normed, axis=-1, keepdims=True)
    return scale * (grad - first - normed * second)


def matmul(a, b):
    return lax.dot_general(a, b, (((1,), (0,)), ((), ())), preferred_element_type=F32)


def matmul_t(a, b):
    return lax.dot_general(a, b, (((1,), (1,)), ((), ())), preferred_element_type=F32)


def col_mask(mask_ref, start, count, pitch, channels):
    row = lax.broadcasted_iota(jnp.int32, (pitch, channels), 0)
    flags = jnp.zeros((pitch, channels), F32)
    for k in range(count):
        flags = jnp.where(row == k, mask_ref[start + k].astype(F32), flags)
    return flags


def load_cells(cells_ref, scratch, first):
    rows, cols, channels = cells_ref.shape
    pitch = pad_to(cols, 16)
    for i in range(rows):
        at = (first + i) * pitch
        scratch[at : at + cols, :] = cells_ref[i].astype(F32)
        if pitch > cols:
            scratch[at + cols : at + pitch, :] = jnp.zeros((pitch - cols, channels), F32)


def row_of(ref, row):
    return ref[pl.ds(row, 8, stride=0), :]


def tiles(value):
    return value.reshape(value.shape[0] // 8, 8, value.shape[1])


def right_kernel(mask_ref, x_ref, w_ref, out_ref, xs):
    rows, cols, channels = x_ref.shape
    pitch = pad_to(cols, 16)
    hidden = w_ref.shape[1] // 4
    load_cells(x_ref, xs, 0)
    normed, _ = normalize(xs[...])
    projected = matmul(normed.astype(BF16), w_ref[:, 2 * hidden :])
    right = jax.nn.sigmoid(projected[:, :hidden]) * projected[:, hidden:]
    flags = col_mask(mask_ref, lax.axis_index("ch") * cols, cols, pitch, hidden)
    start = lax.axis_index("dap") * rows
    for i in range(rows):
        block = slice(i * pitch, (i + 1) * pitch)
        live = flags * mask_ref[start + i].astype(F32)
        out_ref[block, :] = (right[block] * live).astype(BF16)


def left_kernel(mask_ref, x_ref, xp_ref, cot_ref, cotp_ref, w_ref, wg_ref,
                l_ref, lt_ref, gate_ref, cotm_ref, xs, ls, gs):
    rows, cols, channels = x_ref.shape
    pitch = pad_to(cols, 16)
    half = pad_to(rows, 16)
    hidden = w_ref.shape[1] // 4
    dap = lax.axis_index("dap")
    core = lax.rem(dap, 2)
    load_cells(x_ref, xs, 0)
    load_cells(xp_ref, xs, rows)
    normed, _ = normalize(xs[...])
    normed_half = normed.astype(BF16)
    projected = matmul(normed_half, w_ref[:, : 2 * hidden])
    left = jax.nn.sigmoid(projected[:, :hidden]) * projected[:, hidden:]
    flags = col_mask(mask_ref, lax.axis_index("ch") * cols, cols, pitch, hidden)
    for i in range(2 * rows):
        owner = dap if i < rows else dap + 1 - 2 * core
        block = slice(i * pitch, (i + 1) * pitch)
        live = flags * mask_ref[owner * rows + i % rows].astype(F32)
        value = (left[block] * live).astype(BF16).astype(F32)
        l_ref[block, :] = value
        ls[block, :] = value
    tall = pad_to(2 * rows, 16)
    ls[2 * rows * pitch :, :] = jnp.zeros(((tall - 2 * rows) * pitch, hidden), F32)
    for k in range(cols):
        lt_ref[k * tall : (k + 1) * tall, :] = ls[pl.ds(k, tall, stride=pitch), :]
    gs[...] = jax.nn.sigmoid(matmul(normed_half, wg_ref[...]))

    def pick(out_ref):
        for i in range(2 * rows):
            low = gs[i * pitch : i * pitch + rows, :]
            high = gs[i * pitch + rows : i * pitch + 2 * rows, :]
            out_ref[i * half : i * half + rows, :] = jnp.where(core == 0, low, high)
            if half > rows:
                out_ref[i * half + rows : (i + 1) * half, :] = jnp.zeros((half - rows, channels), F32)

    pick(gate_ref)
    load_cells(cot_ref, gs, 0)
    load_cells(cotp_ref, gs, rows)
    pick(cotm_ref)


def factor_kernel(mask_ref, x_ref, w_ref, normed_ref, scale_ref, l1_ref, l2_ref, r1_ref, r2_ref, xs):
    rows, cols, channels = x_ref.shape
    pitch = pad_to(cols, 16)
    hidden = w_ref.shape[1] // 4
    load_cells(x_ref, xs, 0)
    normed, scale = normalize(xs[...])
    normed_ref[...] = normed
    scale_ref[...] = jnp.broadcast_to(scale, normed.shape)
    projected = matmul(normed.astype(BF16), w_ref[...])
    left_sig = jax.nn.sigmoid(projected[:, :hidden])
    right_sig = jax.nn.sigmoid(projected[:, 2 * hidden : 3 * hidden])
    left_in = projected[:, hidden : 2 * hidden] * left_sig * (1.0 - left_sig)
    right_in = projected[:, 3 * hidden :] * right_sig * (1.0 - right_sig)
    flags = col_mask(mask_ref, lax.axis_index("ch") * cols, cols, pitch, hidden)
    start = lax.axis_index("dap") * rows
    for i in range(rows):
        block = slice(i * pitch, (i + 1) * pitch)
        live = flags * mask_ref[start + i].astype(F32)
        l1_ref[block, :] = left_in[block] * live
        l2_ref[block, :] = left_sig[block] * live
        r1_ref[block, :] = right_in[block] * live
        r2_ref[block, :] = right_sig[block] * live


def product_part(lt_ref, r_ref, rs, out, rows, cols):
    pitch, half, tall = pad_to(cols, 16), pad_to(rows, 16), pad_to(2 * rows, 16)
    rs[...] = r_ref[...].astype(F32)

    def step(b, _):
        sums = [jnp.zeros((tall // 8, 8, rs.shape[1]), F32) for _ in range(JB)]
        for k in range(cols):
            left = tiles(lt_ref[k * tall : (k + 1) * tall, :])
            for n in range(JB):
                sums[n] = sums[n] + left * row_of(rs, (b * JB + n) * pitch + k)[None]
        for n in range(JB):
            out[pl.ds(b * JB + n, tall, stride=half), :] = sums[n].reshape(tall, rs.shape[1])
        return 0

    lax.fori_loop(0, rows // JB, step, 0)


def early_kernel(rows, cols, count, *refs):
    lt_ref, shards = refs[0], refs[1 : 1 + count]
    out_ref, rs, ps = refs[1 + count :]
    for s in range(count):
        product_part(lt_ref, shards[s], rs, ps, rows, cols)
        out_ref[s] = ps[: out_ref.shape[1], :].astype(BF16)


def late_kernel(rows, cols, blocks, early, *refs):
    lt_ref, early_ref = refs[:2]
    shards = refs[2 : 2 + blocks - early]
    outs = refs[2 + blocks - early : 2 + 2 * blocks - early]
    rs, ps, held = refs[2 + 2 * blocks - early :]
    chip, column = lax.axis_index("dap") // 2, lax.axis_index("ch")
    for s in range(early):
        held[s] = early_ref[s]
    for s in range(early, blocks):
        product_part(lt_ref, shards[s - early], rs, ps, rows, cols)
        held[s] = ps[: held.shape[1], :].astype(BF16)
    for t in range(blocks):
        outs[t][...] = held[chip ^ column ^ t]


def middle_kernel(blocks, *refs):
    parts = refs[:blocks]
    gate_ref, cot_ref, w_ref, upd_ref, back_ref, logit_ref, gp_ref = refs[blocks:]
    total = parts[0][...].astype(F32)
    for t in range(1, blocks):
        total = total + parts[t][...].astype(F32)
    product = total.astype(BF16).astype(F32)
    hidden_norm, hidden_scale = normalize(product)
    out = matmul(hidden_norm.astype(BF16), w_ref[...])
    gate, upstream = gate_ref[...], cot_ref[...]
    grad_out = (upstream * gate).astype(BF16)
    grad_hidden = matmul_t(grad_out, w_ref[...])
    gp_ref[...] = norm_back(grad_hidden, hidden_norm, hidden_scale).astype(BF16)
    update = (gate * out).astype(BF16)
    logit = (upstream * out * gate * (1.0 - gate)).astype(BF16)
    own = upd_ref.shape[0]
    upd_ref[...] = update[:own]
    logit_ref[...] = logit[:own]
    back_ref[:own, :] = update[own:]
    back_ref[own:, :] = logit[own:]


def grad_right_part(l_ref, piece, store, rows, cols):
    pitch, half = pad_to(cols, 16), pad_to(rows, 16)

    def step(b, _):
        sums = [jnp.zeros((pitch // 8, 8, l_ref.shape[1]), F32) for _ in range(JB)]
        for i in range(2 * rows):
            left = tiles(l_ref[i * pitch : (i + 1) * pitch, :])
            for n in range(JB):
                sums[n] = sums[n] + left * row_of(piece, i * half + b * JB + n)[None]
        for n in range(JB):
            at = pl.multiple_of((b * JB + n) * pitch, pitch)
            store(pl.ds(at, pitch), sums[n].reshape(pitch, l_ref.shape[1]))
        return 0

    lax.fori_loop(0, rows // JB, step, 0)


def send_right_kernel(rows, cols, blocks, s, *refs):
    l_ref, pieces, (out_ref, gs) = refs[0], refs[1 : 1 + blocks], refs[1 + blocks :]
    chip, column = lax.axis_index("dap") // 2, lax.axis_index("ch")
    for t in range(blocks):
        @pl.when(chip ^ column ^ s == t)
        def _(t=t):
            gs[...] = pieces[t][...].astype(F32)

    def store(where, value):
        out_ref[where, :] = value.astype(BF16)

    grad_right_part(l_ref, gs, store, rows, cols)


def grad_left_kernel(rows, cols, blocks, *refs):
    l_ref, pieces, shards = refs[0], refs[1 : 1 + blocks], refs[1 + blocks : 1 + 2 * blocks]
    own_ref, send_ref, right_ref, gs, rs = refs[1 + 2 * blocks :]
    pitch, half = pad_to(cols, 16), pad_to(rows, 16)
    chip = lax.axis_index("dap") // 2
    column = lax.axis_index("ch")
    for t in range(blocks):
        gs[column ^ t] = pieces[t][...].astype(F32)
    for s in range(blocks):
        rs[chip ^ s] = shards[s][...].astype(F32)

    def left_rows(first, ref):
        def step(b, _):
            def block_step(m, sums):
                piece, shard = gs.at[m], rs.at[m]
                sums = list(sums)
                for j in range(rows):
                    right = tiles(shard[j * pitch : (j + 1) * pitch, :])
                    for n in range(JB):
                        row = (first + b * JB + n) * half + j
                        sums[n] = sums[n] + right * row_of(piece, row)[None]
                return tuple(sums)

            zero = jnp.zeros((pitch // 8, 8, gs.shape[2]), F32)
            sums = lax.fori_loop(0, blocks, block_step, (zero,) * JB)
            for n in range(JB):
                at = pl.multiple_of((b * JB + n) * pitch, pitch)
                ref[pl.ds(at, pitch), :] = sums[n].reshape(pitch, gs.shape[2]).astype(ref.dtype)
            return 0

        lax.fori_loop(0, rows // JB, step, 0)

    left_rows(rows, send_ref)
    left_rows(0, own_ref)

    def store(where, value):
        right_ref[where, :] = value

    grad_right_part(l_ref, gs.at[chip], store, rows, cols)


def finish_left_kernel(own_ref, got_ref, l1_ref, l2_ref, w_ref, wg_ref, upd_ref, logit_ref, back_ref,
                       out_ref, acc_ref, us, gs):
    rows, cols, channels = out_ref.shape
    pitch, half = pad_to(cols, 16), pad_to(rows, 16)
    mine = lax.rem(lax.axis_index("dap"), 2) == 0
    for i in range(rows):
        for scratch, ref, base in ((us, upd_ref, 0), (gs, logit_ref, rows * half)):
            here = ref[i * half : (i + 1) * half, :].astype(F32)[:rows]
            there = back_ref[base + i * half : base + (i + 1) * half, :].astype(F32)[:rows]
            scratch[i * pitch : i * pitch + rows, :] = jnp.where(mine, here, there)
            scratch[i * pitch + rows : i * pitch + 2 * rows, :] = jnp.where(mine, there, here)
            if pitch > cols:
                scratch[i * pitch + cols : (i + 1) * pitch, :] = jnp.zeros((pitch - cols, channels), F32)
        out_ref[i] = us[i * pitch : i * pitch + cols, :].astype(BF16)
    grad_left = (own_ref[...] + got_ref[...].astype(F32)).astype(BF16).astype(F32)
    hidden = own_ref.shape[1]
    acc = matmul_t((grad_left * l1_ref[...]).astype(BF16), w_ref[:, :hidden])
    acc = acc + matmul_t((grad_left * l2_ref[...]).astype(BF16), w_ref[:, hidden : 2 * hidden])
    acc_ref[...] = acc + matmul_t(gs[...].astype(BF16), wg_ref[...])


def finish_kernel(blocks, *refs):
    parts = refs[:blocks]
    r1_ref, r2_ref, w_ref, acc_ref, normed_ref, scale_ref, out_ref = refs[blocks:]
    rows, cols, _ = out_ref.shape
    pitch = pad_to(cols, 16)
    total = parts[0][...]
    for s in range(1, blocks):
        total = total + parts[s][...].astype(F32)
    grad_right = total.astype(BF16).astype(F32)
    hidden = total.shape[1]
    grad = acc_ref[...] + matmul_t((grad_right * r1_ref[...]).astype(BF16), w_ref[:, 2 * hidden : 3 * hidden])
    grad = grad + matmul_t((grad_right * r2_ref[...]).astype(BF16), w_ref[:, 3 * hidden :])
    result = norm_back(grad, normed_ref[...], scale_ref[...]).astype(BF16)
    for i in range(rows):
        out_ref[i] = result[i * pitch : i * pitch + cols]


VMEM = pl.BlockSpec(memory_space=pltpu.VMEM)
SMEM = pl.BlockSpec(memory_space=pltpu.SMEM)


def call(body, name, outs, args, scratch=(), smem=0, flops=10**7, limit=20):
    outs = [jax.ShapeDtypeStruct(shape, dtype) for shape, dtype in outs]
    moved = sum(a.size * a.dtype.itemsize for a in list(args) + outs)
    return pl.pallas_call(
        body,
        name=name,
        out_shape=outs,
        in_specs=[SMEM] * smem + [VMEM] * (len(args) - smem),
        out_specs=[VMEM] * len(outs),
        scratch_shapes=[pltpu.VMEM(shape[:-1], BF16) if shape[-1] is None else pltpu.VMEM(shape, F32) for shape in scratch],
        compiler_params=pltpu.CompilerParams(vmem_limit_bytes=limit << 20),
        cost_estimate=pl.CostEstimate(flops=flops, bytes_accessed=moved, transcendentals=0),
    )(*args)


def on_device(devices, blocks, x, mask, w_proj, w_gate, w_out, cot):
    rows, cols, channels = x.shape
    hidden = w_out.shape[0]
    pitch, half, tall = pad_to(cols, 16), pad_to(rows, 16), pad_to(2 * rows, 16)
    cells, wide, mids = rows * pitch, 2 * rows * pitch, 2 * rows * half
    if devices != 2 * blocks or cols != 2 * rows or blocks & (blocks - 1) or rows % JB:
        raise ValueError("unsupported split")

    def along_dap(value, s):
        return lax.ppermute(value, "dap", [(d, d ^ (2 * s)) for d in range(devices)])

    def along_ch(value, t):
        return lax.ppermute(value, "ch", [(h, h ^ t) for h in range(blocks)])

    def to_partner(value):
        return lax.ppermute(value, "dap", [(d, d ^ 1) for d in range(devices)])

    (right,) = call(right_kernel, "right", [((cells, hidden), BF16)], (mask, x, w_proj),
                    [(cells, channels)], smem=1)
    shards = [right] + [along_dap(right, s) for s in range(1, blocks)]
    x_late, cot_late, _ = lax.optimization_barrier((x, cot, right))
    x_pair, cot_pair = to_partner(x_late), to_partner(cot_late)
    left, left_t, gate, upstream = call(
        left_kernel, "left",
        [((wide, hidden), F32), ((cols * tall, hidden), F32), ((mids, channels), F32), ((mids, channels), F32)],
        (mask, x_late, x_pair, cot_late, cot_pair, w_proj, w_gate),
        [(wide, channels), (tall * pitch, hidden), (wide, channels)], smem=1)
    normed, scale, l1, l2, r1, r2 = call(
        factor_kernel, "factor", [((cells, hidden), F32)] * 6, (mask, x_late, w_proj),
        [(cells, channels)], smem=1)
    early = min(EARLY, blocks)
    (started,) = call(functools.partial(early_kernel, rows, cols, early), "early",
                      [((early, mids, hidden), BF16)], (left_t, *shards[:early]), [(cells, hidden), (tall * half, hidden)])
    parts = call(functools.partial(late_kernel, rows, cols, blocks, early), "late",
                 [((mids, hidden), BF16)] * blocks,
                 (left_t, started, *shards[early:]),
                 [(cells, hidden), (tall * half, hidden), (blocks, mids, hidden, None)])
    parts = [parts[0]] + [along_ch(parts[t], t) for t in range(1, blocks)]
    update, back, logit, grad_product = call(
        functools.partial(middle_kernel, blocks), "middle",
        [((mids // 2, channels), BF16), ((mids, channels), BF16), ((mids // 2, channels), BF16), ((mids, hidden), BF16)],
        (*parts, gate, upstream, w_out))
    pieces = [grad_product] + [along_ch(grad_product, t) for t in range(1, blocks)]
    back = to_partner(back)
    gots = [None] * blocks
    for s in [*range(2, blocks), 1]:
        (send,) = call(functools.partial(send_right_kernel, rows, cols, blocks, s), "send_right",
                       [((cells, hidden), BF16)], (left, *pieces), [(mids, hidden)])
        gots[s] = along_dap(send, s)
    left_late, _ = lax.optimization_barrier((left, send))
    left_own, left_send, right_own = call(
        functools.partial(grad_left_kernel, rows, cols, blocks), "grad_left",
        [((cells, hidden), F32), ((cells, hidden), BF16), ((cells, hidden), F32)],
        (left_late, *pieces, *shards), [(blocks, mids, hidden), (blocks, cells, hidden)])
    left_got = to_partner(left_send)
    pair_update, acc = call(
        finish_left_kernel, "finish_left", [((rows, cols, channels), BF16), ((cells, channels), F32)],
        (left_own, left_got, l1, l2, w_proj, w_gate, update, logit, back),
        [(cells, channels), (cells, channels)])
    (grad_pair,) = call(functools.partial(finish_kernel, blocks), "finish", [((rows, cols, channels), BF16)],
                        (right_own, *gots[1:], r1, r2, w_proj, acc, normed, scale))
    return pair_update, grad_pair


def solution(mesh):
    return jax.shard_map(
        functools.partial(on_device, mesh.shape["dap"], mesh.shape["ch"]),
        mesh=mesh,
        in_specs=(P("dap", "ch", None), P(), P(), P(), P(), P("dap", "ch", None)),
        out_specs=(P("dap", "ch", None), P("dap", "ch", None)),
        check_vma=False,
    )
```

```python
import functools

import jax
import jax.numpy as jnp
from jax import lax
from jax.experimental import pallas as pl
from jax.experimental.pallas import tpu as pltpu
from jax.sharding import PartitionSpec as P


EPSILON = 1e-05
F32 = jnp.float32
BF16 = jnp.bfloat16
JB = 5


def pad_to(count, tile):
    return (count + tile - 1) // tile * tile


def normalize(values):
    center = jnp.mean(values, axis=-1, keepdims=True)
    spread = values - center
    scale = lax.rsqrt(jnp.mean(spread * spread, axis=-1, keepdims=True) + EPSILON)
    return spread * scale, scale


def norm_back(grad, normed, scale):
    first = jnp.mean(grad, axis=-1, keepdims=True)
    second = jnp.mean(grad * normed, axis=-1, keepdims=True)
    return scale * (grad - first - normed * second)


def matmul(a, b):
    return lax.dot_general(a, b, (((1,), (0,)), ((), ())), preferred_element_type=F32)


def matmul_t(a, b):
    return lax.dot_general(a, b, (((1,), (1,)), ((), ())), preferred_element_type=F32)


def load_kernel(*refs):
    count = len(refs) // 2 - 1
    sources, outs, (sems, flags) = refs[:count], refs[count : 2 * count], refs[2 * count :]
    live_ref = outs[-1]
    copies = [pltpu.make_async_copy(sources[0], flags, sems.at[0])]
    copies += [pltpu.make_async_copy(a, b, sems.at[n + 1]) for n, (a, b) in enumerate(zip(sources[1:], outs[:-1]))]
    for copy in copies:
        copy.start()
    copies[0].wait()
    residues, total = flags.shape[0], live_ref.shape[0]
    for r in range(residues):
        live_ref[r : r + 1, :] = jnp.full((1, live_ref.shape[1]), flags[r].astype(F32))
    live_ref[residues:, :] = jnp.zeros((total - residues, live_ref.shape[1]), F32)
    for copy in copies[1:]:
        copy.wait()


def live_rows(live_ref, start, first, rows, pitch):
    columns = tiles(live_ref[pl.ds(first, pitch), :])
    for i in range(rows):
        yield i, (columns * row_of(live_ref, start + i)[None]).reshape(pitch, columns.shape[2])


def load_cells(cells_ref, scratch, first):
    rows, cols, channels = cells_ref.shape
    pitch = pad_to(cols, 16)
    for i in range(rows):
        at = (first + i) * pitch
        scratch[at : at + cols, :] = cells_ref[i].astype(F32)
        if pitch > cols:
            scratch[at + cols : at + pitch, :] = jnp.zeros((pitch - cols, channels), F32)


def row_of(ref, row):
    return ref[pl.ds(row, 8, stride=0), :]


def tiles(value):
    return value.reshape(value.shape[0] // 8, 8, value.shape[1])


def left_kernel(live_ref, x_ref, xp_ref, cot_ref, cotp_ref, w_ref, wg_ref,
                l_ref, lt_ref, gate_ref, cotm_ref, xs, ls, gs):
    rows, cols, channels = x_ref.shape
    pitch = pad_to(cols, 16)
    half = pad_to(rows, 16)
    hidden = w_ref.shape[1] // 4
    dap = lax.axis_index("dap")
    core = lax.rem(dap, 2)
    load_cells(x_ref, xs, 0)
    load_cells(xp_ref, xs, rows)
    normed, _ = normalize(xs[...])
    normed_half = normed.astype(BF16)
    projected = matmul(normed_half, w_ref[:, : 2 * hidden])
    left = jax.nn.sigmoid(projected[:, :hidden]) * projected[:, hidden:]
    for part, owner in enumerate((dap, dap + 1 - 2 * core)):
        for i, live in live_rows(live_ref, owner * rows, lax.axis_index("ch") * cols, rows, pitch):
            block = slice((part * rows + i) * pitch, (part * rows + i + 1) * pitch)
            value = (left[block] * live).astype(BF16).astype(F32)
            l_ref[block, :] = value
            ls[block, :] = value
    tall = pad_to(2 * rows, 16)
    ls[2 * rows * pitch :, :] = jnp.zeros(((tall - 2 * rows) * pitch, hidden), F32)
    for k in range(cols):
        lt_ref[k * tall : (k + 1) * tall, :] = ls[pl.ds(k, tall, stride=pitch), :]
    gs[...] = jax.nn.sigmoid(matmul(normed_half, wg_ref[...]))

    def pick(out_ref):
        for i in range(2 * rows):
            low = gs[i * pitch : i * pitch + rows, :]
            high = gs[i * pitch + rows : i * pitch + 2 * rows, :]
            out_ref[i * half : i * half + rows, :] = jnp.where(core == 0, low, high)
            if half > rows:
                out_ref[i * half + rows : (i + 1) * half, :] = jnp.zeros((half - rows, channels), F32)

    pick(gate_ref)
    load_cells(cot_ref, gs, 0)
    load_cells(cotp_ref, gs, rows)
    pick(cotm_ref)


def factor_kernel(live_ref, x_ref, w_ref, normed_ref, scale_ref, l1_ref, l2_ref, r1_ref, r2_ref, xs):
    rows, cols, _ = x_ref.shape
    pitch = pad_to(cols, 16)
    hidden = w_ref.shape[1] // 4
    load_cells(x_ref, xs, 0)
    normed, scale = normalize(xs[...])
    normed_ref[...] = normed
    scale_ref[...] = jnp.broadcast_to(scale, normed.shape)
    projected = matmul(normed.astype(BF16), w_ref[...])
    left_sig = jax.nn.sigmoid(projected[:, :hidden])
    right_sig = jax.nn.sigmoid(projected[:, 2 * hidden : 3 * hidden])
    left_in = projected[:, hidden : 2 * hidden] * left_sig * (1.0 - left_sig)
    right_in = projected[:, 3 * hidden :] * right_sig * (1.0 - right_sig)
    start = lax.axis_index("dap") * rows
    for i, live in live_rows(live_ref, start, lax.axis_index("ch") * cols, rows, pitch):
        block = slice(i * pitch, (i + 1) * pitch)
        l1_ref[block, :] = left_in[block] * live
        l2_ref[block, :] = left_sig[block] * live
        r1_ref[block, :] = right_in[block] * live
        r2_ref[block, :] = right_sig[block] * live


def product_part(lt_ref, rs, out, rows, cols):
    pitch, half, tall = pad_to(cols, 16), pad_to(rows, 16), pad_to(2 * rows, 16)

    def step(b, _):
        sums = [jnp.zeros((tall // 8, 8, rs.shape[1]), F32) for _ in range(JB)]
        for k in range(cols):
            left = tiles(lt_ref[k * tall : (k + 1) * tall, :])
            for n in range(JB):
                sums[n] = sums[n] + left * row_of(rs, (b * JB + n) * pitch + k)[None]
        for n in range(JB):
            out[pl.ds(b * JB + n, tall, stride=half), :] = sums[n].reshape(tall, rs.shape[1])
        return 0

    lax.fori_loop(0, rows // JB, step, 0)


def right_of(live_ref, x_ref, w_ref, xs, rs, r_ref, s):
    rows, cols, _ = x_ref.shape
    pitch = pad_to(cols, 16)
    hidden = w_ref.shape[1] // 4
    load_cells(x_ref, xs, 0)
    normed, _ = normalize(xs[...])
    projected = matmul(normed.astype(BF16), w_ref[:, 2 * hidden :])
    right = jax.nn.sigmoid(projected[:, :hidden]) * projected[:, hidden:]
    start = (lax.axis_index("dap") ^ (2 * s)) * rows
    for i, live in live_rows(live_ref, start, lax.axis_index("ch") * cols, rows, pitch):
        block = slice(i * pitch, (i + 1) * pitch)
        value = (right[block] * live).astype(BF16)
        r_ref[block, :] = value
        rs[block, :] = value.astype(F32)


def part_kernel(step, live_ref, lt_ref, w_ref, shard, right_ref, part_ref, xs, rs, ps):
    rows, cols, _ = shard.shape
    right_of(live_ref, shard, w_ref, xs, rs, right_ref, step)
    product_part(lt_ref, rs, ps, rows, cols)
    part_ref[...] = ps[: part_ref.shape[0], :].astype(BF16)


def late_kernel(blocks, step, *refs):
    live_ref, lt_ref, w_ref, shard = refs[:4]
    done = refs[4 : 3 + blocks]
    right_ref, outs = refs[3 + blocks], refs[4 + blocks : 4 + 2 * blocks]
    xs, rs, ps, held = refs[4 + 2 * blocks :]
    rows, cols, _ = shard.shape
    for s in range(blocks):
        if s != step:
            held[s] = done[s - (s > step)][...]
    right_of(live_ref, shard, w_ref, xs, rs, right_ref, step)
    product_part(lt_ref, rs, ps, rows, cols)
    held[step] = ps[: held.shape[1], :].astype(BF16)
    turn = (lax.axis_index("dap") // 2) ^ lax.axis_index("ch")
    for t in range(blocks):
        outs[t][...] = held[turn ^ t]


def middle_kernel(blocks, *refs):
    parts = refs[:blocks]
    gate_ref, cot_ref, w_ref, upd_ref, back_ref, logit_ref, gp_ref = refs[blocks:]
    total = parts[0][...].astype(F32)
    for t in range(1, blocks):
        total = total + parts[t][...].astype(F32)
    product = total.astype(BF16).astype(F32)
    hidden_norm, hidden_scale = normalize(product)
    out = matmul(hidden_norm.astype(BF16), w_ref[...])
    gate, upstream = gate_ref[...], cot_ref[...]
    grad_out = (upstream * gate).astype(BF16)
    grad_hidden = matmul_t(grad_out, w_ref[...])
    gp_ref[...] = norm_back(grad_hidden, hidden_norm, hidden_scale).astype(BF16)
    update = (gate * out).astype(BF16)
    logit = (upstream * out * gate * (1.0 - gate)).astype(BF16)
    own = upd_ref.shape[0]
    upd_ref[...] = update[:own]
    logit_ref[...] = logit[:own]
    back_ref[:own, :] = update[own:]
    back_ref[own:, :] = logit[own:]


def grad_right_part(l_ref, piece, store, rows, cols):
    pitch, half = pad_to(cols, 16), pad_to(rows, 16)

    def step(b, _):
        sums = [jnp.zeros((pitch // 8, 8, l_ref.shape[1]), F32) for _ in range(JB)]
        for i in range(2 * rows):
            left = tiles(l_ref[i * pitch : (i + 1) * pitch, :])
            for n in range(JB):
                sums[n] = sums[n] + left * row_of(piece, i * half + b * JB + n)[None]
        for n in range(JB):
            at = pl.multiple_of((b * JB + n) * pitch, pitch)
            store(pl.ds(at, pitch), sums[n].reshape(pitch, l_ref.shape[1]))
        return 0

    lax.fori_loop(0, rows // JB, step, 0)


def send_right_kernel(rows, cols, blocks, s, *refs):
    l_ref, pieces, (out_ref, gs) = refs[0], refs[1 : 1 + blocks], refs[1 + blocks :]
    chip, column = lax.axis_index("dap") // 2, lax.axis_index("ch")
    for t in range(blocks):
        @pl.when(chip ^ column ^ s == t)
        def _(t=t):
            gs[...] = pieces[t][...].astype(F32)

    def store(where, value):
        out_ref[where, :] = value.astype(BF16)

    grad_right_part(l_ref, gs, store, rows, cols)


def grad_left_kernel(rows, cols, blocks, *refs):
    l_ref, pieces, shards = refs[0], refs[1 : 1 + blocks], refs[1 + blocks : 1 + 2 * blocks]
    own_ref, send_ref, right_ref, gs, rs = refs[1 + 2 * blocks :]
    pitch, half = pad_to(cols, 16), pad_to(rows, 16)
    chip = lax.axis_index("dap") // 2
    column = lax.axis_index("ch")
    for t in range(blocks):
        gs[column ^ t] = pieces[t][...].astype(F32)
    for s in range(blocks):
        rs[chip ^ s] = shards[s][...].astype(F32)

    def left_rows(first, ref):
        def step(b, _):
            def block_step(m, sums):
                piece, shard = gs.at[m], rs.at[m]
                sums = list(sums)
                for j in range(rows):
                    right = tiles(shard[j * pitch : (j + 1) * pitch, :])
                    for n in range(JB):
                        row = (first + b * JB + n) * half + j
                        sums[n] = sums[n] + right * row_of(piece, row)[None]
                return tuple(sums)

            zero = jnp.zeros((pitch // 8, 8, gs.shape[2]), F32)
            sums = lax.fori_loop(0, blocks, block_step, (zero,) * JB)
            for n in range(JB):
                at = pl.multiple_of((b * JB + n) * pitch, pitch)
                ref[pl.ds(at, pitch), :] = sums[n].reshape(pitch, gs.shape[2]).astype(ref.dtype)
            return 0

        lax.fori_loop(0, rows // JB, step, 0)

    left_rows(rows, send_ref)
    left_rows(0, own_ref)

    def store(where, value):
        right_ref[where, :] = value

    grad_right_part(l_ref, gs.at[chip], store, rows, cols)


def finish_left_kernel(own_ref, got_ref, l1_ref, l2_ref, w_ref, wg_ref, upd_ref, logit_ref, back_ref,
                       out_ref, acc_ref, us, gs):
    rows, cols, channels = out_ref.shape
    pitch, half = pad_to(cols, 16), pad_to(rows, 16)
    mine = lax.rem(lax.axis_index("dap"), 2) == 0
    for i in range(rows):
        for scratch, ref, base in ((us, upd_ref, 0), (gs, logit_ref, rows * half)):
            here = ref[i * half : (i + 1) * half, :].astype(F32)[:rows]
            there = back_ref[base + i * half : base + (i + 1) * half, :].astype(F32)[:rows]
            scratch[i * pitch : i * pitch + rows, :] = jnp.where(mine, here, there)
            scratch[i * pitch + rows : i * pitch + 2 * rows, :] = jnp.where(mine, there, here)
            if pitch > cols:
                scratch[i * pitch + cols : (i + 1) * pitch, :] = jnp.zeros((pitch - cols, channels), F32)
        out_ref[i] = us[i * pitch : i * pitch + cols, :].astype(BF16)
    grad_left = (own_ref[...] + got_ref[...].astype(F32)).astype(BF16).astype(F32)
    hidden = own_ref.shape[1]
    acc = matmul_t((grad_left * l1_ref[...]).astype(BF16), w_ref[:, :hidden])
    acc = acc + matmul_t((grad_left * l2_ref[...]).astype(BF16), w_ref[:, hidden : 2 * hidden])
    acc_ref[...] = acc + matmul_t(gs[...].astype(BF16), wg_ref[...])


def finish_kernel(blocks, *refs):
    parts = refs[:blocks]
    r1_ref, r2_ref, w_ref, acc_ref, normed_ref, scale_ref, out_ref = refs[blocks:]
    rows, cols, _ = out_ref.shape
    pitch = pad_to(cols, 16)
    total = parts[0][...]
    for s in range(1, blocks):
        total = total + parts[s][...].astype(F32)
    grad_right = total.astype(BF16).astype(F32)
    hidden = total.shape[1]
    grad = acc_ref[...] + matmul_t((grad_right * r1_ref[...]).astype(BF16), w_ref[:, 2 * hidden : 3 * hidden])
    grad = grad + matmul_t((grad_right * r2_ref[...]).astype(BF16), w_ref[:, 3 * hidden :])
    result = norm_back(grad, normed_ref[...], scale_ref[...]).astype(BF16)
    for i in range(rows):
        out_ref[i] = result[i * pitch : i * pitch + cols]


VMEM = pl.BlockSpec(memory_space=pltpu.VMEM)
HBM = pl.BlockSpec(memory_space=pltpu.HBM)


def call(body, outs, args, scratch=(), specs=VMEM, flops=10**7):
    outs = [jax.ShapeDtypeStruct(shape, dtype) for shape, dtype in outs]
    moved = sum(a.size * a.dtype.itemsize for a in [*args, *outs])
    scratch = [pltpu.VMEM(shape, F32) if isinstance(shape, tuple) else shape for shape in scratch]
    return pl.pallas_call(
        body,
        out_shape=outs,
        in_specs=[specs] * len(args),
        out_specs=[VMEM] * len(outs),
        scratch_shapes=scratch,
        compiler_params=pltpu.CompilerParams(vmem_limit_bytes=20 << 20),
        cost_estimate=pl.CostEstimate(flops=flops, bytes_accessed=moved, transcendentals=0),
    )(*args)


def on_device(devices, blocks, x, mask, w_proj, w_gate, w_out, cot):
    rows, cols, channels = x.shape
    hidden = w_out.shape[0]
    pitch, half, tall = pad_to(cols, 16), pad_to(rows, 16), pad_to(2 * rows, 16)
    cells, wide, mids = rows * pitch, 2 * rows * pitch, 2 * rows * half
    if devices != 2 * blocks or cols != 2 * rows or blocks & (blocks - 1) or rows % JB:
        raise ValueError("unsupported split")

    def along_dap(value, s):
        return lax.ppermute(value, "dap", [(d, d ^ (2 * s)) for d in range(devices)])

    def along_ch(value, t):
        return lax.ppermute(value, "ch", [(h, h ^ t) for h in range(blocks)])

    def to_partner(value):
        return lax.ppermute(value, "dap", [(d, d ^ 1) for d in range(devices)])

    last = blocks - 1
    shards = [x] + [None] * last
    for s in dap_order(blocks):
        direct = s == 1 or s % 2 == 0
        shards[s] = along_dap(x if direct else shards[s ^ 1], s if direct else 1)
    x_pair, cot_pair = to_partner(x), to_partner(cot)
    sources = (x, cot, w_proj, w_gate, w_out)
    residues = mask.shape[0]
    xv, cotv, w_proj, w_gate, w_out, live = call(
        load_kernel,
        [(a.shape, a.dtype) for a in sources] + [((pad_to(residues + pitch - cols, 8), channels), F32)],
        [pltpu.with_memory_space_constraint(a, pltpu.HBM) for a in (mask, *sources)], [pltpu.SemaphoreType.DMA((6,)), pltpu.SMEM((residues,), jnp.int32)], specs=HBM)
    left, left_t, gate, upstream = call(
        left_kernel,
        [((wide, hidden), F32), ((cols * tall, hidden), F32), ((mids, channels), F32), ((mids, channels), F32)],
        (live, xv, x_pair, cotv, cot_pair, w_proj, w_gate),
        [(wide, channels), (tall * pitch, hidden), (wide, channels)])
    scratch = [(cells, channels), (cells, hidden), (tall * half, hidden)]
    rights, done = [None] * blocks, []
    for s in range(last):
        rights[s], part = call(
            functools.partial(part_kernel, s), [((cells, hidden), BF16), ((mids, hidden), BF16)],
            (live, left_t, w_proj, shards[s] if s else xv), scratch)
        done.append(part)
    rights[last], *parts = call(
        functools.partial(late_kernel, blocks, last),
        [((cells, hidden), BF16)] + [((mids, hidden), BF16)] * blocks,
        (live, left_t, w_proj, shards[last], *done), scratch + [pltpu.VMEM((blocks, mids, hidden), BF16)])
    for t in range(1, blocks):
        parts[t] = along_ch(parts[t], t)
    update, back, logit, grad_product = call(
        functools.partial(middle_kernel, blocks),
        [((mids // 2, channels), BF16), ((mids, channels), BF16), ((mids // 2, channels), BF16), ((mids, hidden), BF16)],
        (*parts, gate, upstream, w_out))
    pieces = [grad_product] + [along_ch(grad_product, t) for t in range(1, blocks)]
    back = to_partner(back)
    gots = [None] * blocks
    for s in range(1, blocks):
        (send,) = call(functools.partial(send_right_kernel, rows, cols, blocks, s),
                       [((cells, hidden), BF16)], (left, *pieces), [(mids, hidden)])
        gots[s] = along_dap(send, s)
    left_own, left_send, right_own = call(
        functools.partial(grad_left_kernel, rows, cols, blocks),
        [((cells, hidden), F32), ((cells, hidden), BF16), ((cells, hidden), F32)],
        (left, *pieces, *rights), [(blocks, mids, hidden), (blocks, cells, hidden)])
    left_got = to_partner(left_send)
    normed, scale, l1, l2, r1, r2 = call(
        factor_kernel, [((cells, hidden), F32)] * 6, (live, xv, w_proj),
        [(cells, channels)])
    pair_update, acc = call(
        finish_left_kernel, [((rows, cols, channels), BF16), ((cells, channels), F32)],
        (left_own, left_got, l1, l2, w_proj, w_gate, update, logit, back),
        [(cells, channels), (cells, channels)])
    (grad_pair,) = call(functools.partial(finish_kernel, blocks), [((rows, cols, channels), BF16)],
                        (right_own, *gots[1:], r1, r2, w_proj, acc, normed, scale))
    return pair_update, grad_pair


def dap_order(blocks):
    return [*range(2, blocks, 2), 1, *range(3, blocks, 2)]


def solution(mesh):
    blocks = mesh.shape["ch"]

    def body(*args):
        return on_device(mesh.shape["dap"], blocks, *args)

    return jax.shard_map(
        body,
        mesh=mesh,
        in_specs=(P("dap", "ch", None), P(), P(), P(), P(), P("dap", "ch", None)),
        out_specs=(P("dap", "ch", None), P("dap", "ch", None)),
        check_vma=False,
    )
```

```python
import functools

import jax
import jax.numpy as jnp
from jax import lax
from jax.experimental import pallas as pl
from jax.experimental.pallas import tpu as pltpu
from jax.sharding import PartitionSpec as P


EPSILON = 1e-05
F32 = jnp.float32
BF16 = jnp.bfloat16
JB = 5


def pad_to(count, tile):
    return (count + tile - 1) // tile * tile


def normalize(values):
    center = jnp.mean(values, axis=-1, keepdims=True)
    spread = values - center
    scale = lax.rsqrt(jnp.mean(spread * spread, axis=-1, keepdims=True) + EPSILON)
    return spread * scale, scale


def norm_back(grad, normed, scale):
    first = jnp.mean(grad, axis=-1, keepdims=True)
    second = jnp.mean(grad * normed, axis=-1, keepdims=True)
    return scale * (grad - first - normed * second)


def matmul(a, b):
    return lax.dot_general(a, b, (((1,), (0,)), ((), ())), preferred_element_type=F32)


def matmul_t(a, b):
    return lax.dot_general(a, b, (((1,), (1,)), ((), ())), preferred_element_type=F32)


def load_kernel(*refs):
    count = len(refs) // 2 - 1
    sources, outs, (sems, flags) = refs[:count], refs[count : 2 * count], refs[2 * count :]
    live_ref = outs[-1]
    copies = [pltpu.make_async_copy(sources[0], flags, sems.at[0])]
    copies += [pltpu.make_async_copy(a, b, sems.at[n + 1]) for n, (a, b) in enumerate(zip(sources[1:], outs[:-1]))]
    for copy in copies:
        copy.start()
    copies[0].wait()
    residues, total = flags.shape[0], live_ref.shape[0]
    for r in range(residues):
        live_ref[r : r + 1, :] = jnp.full((1, live_ref.shape[1]), flags[r].astype(F32))
    live_ref[residues:, :] = jnp.zeros((total - residues, live_ref.shape[1]), F32)
    for copy in copies[1:]:
        copy.wait()


def live_rows(live_ref, start, first, rows, pitch):
    columns = tiles(live_ref[pl.ds(first, pitch), :])
    for i in range(rows):
        yield i, (columns * row_of(live_ref, start + i)[None]).reshape(pitch, columns.shape[2])


def load_cells(cells_refs, scratch, first):
    rows, cols, channels = cells_refs[0].shape
    pitch = pad_to(cols, 16)
    for i in range(rows):
        at = (first + i) * pitch
        scratch[at : at + cols, :] = sum(ref[i].astype(F32) for ref in cells_refs)
        if pitch > cols:
            scratch[at + cols : at + pitch, :] = jnp.zeros((pitch - cols, channels), F32)


def row_of(ref, row):
    return ref[pl.ds(row, 8, stride=0), :]


def tiles(value):
    return value.reshape(value.shape[0] // 8, 8, value.shape[1])


def left_kernel(live_ref, x_ref, xp_ref, cot_ref, cotp_ref, w_ref, wg_ref,
                l_ref, lt_ref, gate_ref, cotm_ref, xs, ls, gs):
    rows, cols, channels = x_ref.shape
    pitch = pad_to(cols, 16)
    half = pad_to(rows, 16)
    hidden = w_ref.shape[1] // 4
    dap = lax.axis_index("dap")
    core = lax.rem(dap, 2)
    load_cells([x_ref], xs, 0)
    load_cells([xp_ref], xs, rows)
    normed, _ = normalize(xs[...])
    normed_half = normed.astype(BF16)
    projected = matmul(normed_half, w_ref[:, : 2 * hidden])
    left = jax.nn.sigmoid(projected[:, :hidden]) * projected[:, hidden:]
    for part, owner in enumerate((dap, dap + 1 - 2 * core)):
        for i, live in live_rows(live_ref, owner * rows, lax.axis_index("ch") * cols, rows, pitch):
            block = slice((part * rows + i) * pitch, (part * rows + i + 1) * pitch)
            value = (left[block] * live).astype(BF16).astype(F32)
            l_ref[block, :] = value
            ls[block, :] = value
    tall = pad_to(2 * rows, 16)
    ls[2 * rows * pitch :, :] = jnp.zeros(((tall - 2 * rows) * pitch, hidden), F32)
    for k in range(cols):
        lt_ref[k * tall : (k + 1) * tall, :] = ls[pl.ds(k, tall, stride=pitch), :]
    gs[...] = jax.nn.sigmoid(matmul(normed_half, wg_ref[...]))

    def pick(out_ref):
        for i in range(2 * rows):
            low = gs[i * pitch : i * pitch + rows, :]
            high = gs[i * pitch + rows : i * pitch + 2 * rows, :]
            out_ref[i * half : i * half + rows, :] = jnp.where(core == 0, low, high)
            if half > rows:
                out_ref[i * half + rows : (i + 1) * half, :] = jnp.zeros((half - rows, channels), F32)

    pick(gate_ref)
    load_cells([cot_ref], gs, 0)
    load_cells([cotp_ref], gs, rows)
    pick(cotm_ref)


def factor_kernel(live_ref, x_ref, w_ref, normed_ref, scale_ref, l1_ref, l2_ref, r1_ref, r2_ref, xs):
    rows, cols, _ = x_ref.shape
    pitch = pad_to(cols, 16)
    hidden = w_ref.shape[1] // 4
    load_cells([x_ref], xs, 0)
    normed, scale = normalize(xs[...])
    normed_ref[...] = normed
    scale_ref[...] = jnp.broadcast_to(scale, normed.shape)
    projected = matmul(normed.astype(BF16), w_ref[...])
    left_sig = jax.nn.sigmoid(projected[:, :hidden])
    right_sig = jax.nn.sigmoid(projected[:, 2 * hidden : 3 * hidden])
    left_in = projected[:, hidden : 2 * hidden] * left_sig * (1.0 - left_sig)
    right_in = projected[:, 3 * hidden :] * right_sig * (1.0 - right_sig)
    start = lax.axis_index("dap") * rows
    for i, live in live_rows(live_ref, start, lax.axis_index("ch") * cols, rows, pitch):
        block = slice(i * pitch, (i + 1) * pitch)
        l1_ref[block, :] = left_in[block] * live
        l2_ref[block, :] = left_sig[block] * live
        r1_ref[block, :] = right_in[block] * live
        r2_ref[block, :] = right_sig[block] * live


def product_part(lt_ref, rs, out, rows, cols):
    pitch, half, tall = pad_to(cols, 16), pad_to(rows, 16), pad_to(2 * rows, 16)

    def step(b, _):
        sums = [jnp.zeros((tall // 8, 8, rs.shape[1]), F32) for _ in range(JB)]
        for k in range(cols):
            left = tiles(lt_ref[k * tall : (k + 1) * tall, :])
            for n in range(JB):
                sums[n] = sums[n] + left * row_of(rs, (b * JB + n) * pitch + k)[None]
        for n in range(JB):
            out[pl.ds(b * JB + n, tall, stride=half), :] = sums[n].reshape(tall, rs.shape[1])
        return 0

    lax.fori_loop(0, rows // JB, step, 0)


def lookup(table, chip):
    value = table[0]
    for z in range(1, len(table)):
        if table[z] != table[0]:
            value = jnp.where(chip == z, table[z], value)
    return value


def this_chip():
    return lax.axis_index("dap") // 2


def right_of(live_ref, x_refs, w_ref, xs, rs, r_ref, s):
    rows, cols, _ = x_refs[0].shape
    pitch = pad_to(cols, 16)
    hidden = w_ref.shape[1] // 4
    load_cells(x_refs, xs, 0)
    normed, _ = normalize(xs[...])
    projected = matmul(normed.astype(BF16), w_ref[:, 2 * hidden :])
    right = jax.nn.sigmoid(projected[:, :hidden]) * projected[:, hidden:]
    start = (lax.axis_index("dap") ^ (2 * s)) * rows
    for i, live in live_rows(live_ref, start, lax.axis_index("ch") * cols, rows, pitch):
        block = slice(i * pitch, (i + 1) * pitch)
        value = (right[block] * live).astype(BF16)
        r_ref[block, :] = value
        rs[block, :] = value.astype(F32)


def part_kernel(steps, live_ref, lt_ref, w_ref, *refs):
    shards, (right_ref, part_ref, xs, rs, ps) = refs[:-5], refs[-5:]
    rows, cols, _ = shards[0].shape
    right_of(live_ref, shards, w_ref, xs, rs, right_ref, lookup(steps, this_chip()))
    product_part(lt_ref, rs, ps, rows, cols)
    part_ref[...] = ps[: part_ref.shape[0], :].astype(BF16)


def late_kernel(steps, live_ref, lt_ref, w_ref, *refs):
    blocks = len(steps)
    done, refs = refs[: blocks - 1], refs[blocks - 1 :]
    split = len(refs) - blocks - 5
    shards, right_ref, outs, (xs, rs, ps, held) = refs[:split], refs[split], refs[split + 1 : -4], refs[-4:]
    rows, cols, _ = shards[0].shape
    chip = this_chip()
    for part, table in zip(done, steps):
        held[lookup(table, chip)] = part[...]
    last = lookup(steps[-1], chip)
    right_of(live_ref, shards, w_ref, xs, rs, right_ref, last)
    product_part(lt_ref, rs, ps, rows, cols)
    held[last] = ps[: held.shape[1], :].astype(BF16)
    turn = chip ^ lax.axis_index("ch")
    for t in range(blocks):
        outs[t][...] = held[turn ^ t]


def middle_kernel(blocks, *refs):
    parts = refs[:blocks]
    gate_ref, cot_ref, w_ref, upd_ref, back_ref, logit_ref, gp_ref = refs[blocks:]
    total = parts[0][...].astype(F32)
    for t in range(1, blocks):
        total = total + parts[t][...].astype(F32)
    product = total.astype(BF16).astype(F32)
    hidden_norm, hidden_scale = normalize(product)
    out = matmul(hidden_norm.astype(BF16), w_ref[...])
    gate, upstream = gate_ref[...], cot_ref[...]
    grad_out = (upstream * gate).astype(BF16)
    grad_hidden = matmul_t(grad_out, w_ref[...])
    gp_ref[...] = norm_back(grad_hidden, hidden_norm, hidden_scale).astype(BF16)
    update = (gate * out).astype(BF16)
    logit = (upstream * out * gate * (1.0 - gate)).astype(BF16)
    own = upd_ref.shape[0]
    upd_ref[...] = update[:own]
    logit_ref[...] = logit[:own]
    back_ref[:own, :] = update[own:]
    back_ref[own:, :] = logit[own:]


def grad_right_part(l_ref, piece, store, rows, cols):
    pitch, half = pad_to(cols, 16), pad_to(rows, 16)

    def step(b, _):
        sums = [jnp.zeros((pitch // 8, 8, l_ref.shape[1]), F32) for _ in range(JB)]
        for i in range(2 * rows):
            left = tiles(l_ref[i * pitch : (i + 1) * pitch, :])
            for n in range(JB):
                sums[n] = sums[n] + left * row_of(piece, i * half + b * JB + n)[None]
        for n in range(JB):
            at = pl.multiple_of((b * JB + n) * pitch, pitch)
            store(pl.ds(at, pitch), sums[n].reshape(pitch, l_ref.shape[1]))
        return 0

    lax.fori_loop(0, rows // JB, step, 0)


def send_right_kernel(rows, cols, blocks, steps, *refs):
    l_ref, pieces = refs[0], refs[1 : 1 + blocks]
    more, (out_ref, gs) = refs[1 + blocks : -2], refs[-2:]
    chip, column = this_chip(), lax.axis_index("ch")
    step = lookup(steps, chip)
    for t in range(blocks):
        @pl.when(chip ^ column ^ step == t)
        def _(t=t):
            gs[...] = pieces[t][...].astype(F32)

    def store(where, value):
        for ref in more:
            value = value + ref[where, :].astype(F32)
        out_ref[where, :] = value.astype(BF16)

    grad_right_part(l_ref, gs, store, rows, cols)


def grad_left_kernel(rows, cols, steps, *refs):
    blocks = len(steps)
    l_ref, pieces, shards = refs[0], refs[1 : 1 + blocks], refs[1 + blocks : 1 + 2 * blocks]
    own_ref, send_ref, right_ref, gs, rs = refs[1 + 2 * blocks :]
    pitch, half = pad_to(cols, 16), pad_to(rows, 16)
    chip = lax.axis_index("dap") // 2
    column = lax.axis_index("ch")
    for t in range(blocks):
        gs[column ^ t] = pieces[t][...].astype(F32)
    for table, shard in zip(steps, shards):
        rs[chip ^ lookup(table, chip)] = shard[...].astype(F32)

    def left_rows(first, ref):
        def step(b, _):
            def block_step(m, sums):
                piece, shard = gs.at[m], rs.at[m]
                sums = list(sums)
                for j in range(rows):
                    right = tiles(shard[j * pitch : (j + 1) * pitch, :])
                    for n in range(JB):
                        row = (first + b * JB + n) * half + j
                        sums[n] = sums[n] + right * row_of(piece, row)[None]
                return tuple(sums)

            zero = jnp.zeros((pitch // 8, 8, gs.shape[2]), F32)
            sums = lax.fori_loop(0, blocks, block_step, (zero,) * JB)
            for n in range(JB):
                at = pl.multiple_of((b * JB + n) * pitch, pitch)
                ref[pl.ds(at, pitch), :] = sums[n].reshape(pitch, gs.shape[2]).astype(ref.dtype)
            return 0

        lax.fori_loop(0, rows // JB, step, 0)

    left_rows(rows, send_ref)
    left_rows(0, own_ref)

    def store(where, value):
        right_ref[where, :] = value

    grad_right_part(l_ref, gs.at[chip], store, rows, cols)


def finish_left_kernel(own_ref, got_ref, l1_ref, l2_ref, w_ref, wg_ref, upd_ref, logit_ref, back_ref,
                       out_ref, acc_ref, us, gs):
    rows, cols, channels = out_ref.shape
    pitch, half = pad_to(cols, 16), pad_to(rows, 16)
    mine = lax.rem(lax.axis_index("dap"), 2) == 0
    for i in range(rows):
        for scratch, ref, base in ((us, upd_ref, 0), (gs, logit_ref, rows * half)):
            here = ref[i * half : (i + 1) * half, :].astype(F32)[:rows]
            there = back_ref[base + i * half : base + (i + 1) * half, :].astype(F32)[:rows]
            scratch[i * pitch : i * pitch + rows, :] = jnp.where(mine, here, there)
            scratch[i * pitch + rows : i * pitch + 2 * rows, :] = jnp.where(mine, there, here)
            if pitch > cols:
                scratch[i * pitch + cols : (i + 1) * pitch, :] = jnp.zeros((pitch - cols, channels), F32)
        out_ref[i] = us[i * pitch : i * pitch + cols, :].astype(BF16)
    grad_left = (own_ref[...] + got_ref[...].astype(F32)).astype(BF16).astype(F32)
    hidden = own_ref.shape[1]
    acc = matmul_t((grad_left * l1_ref[...]).astype(BF16), w_ref[:, :hidden])
    acc = acc + matmul_t((grad_left * l2_ref[...]).astype(BF16), w_ref[:, hidden : 2 * hidden])
    acc_ref[...] = acc + matmul_t(gs[...].astype(BF16), wg_ref[...])


def finish_kernel(count, *refs):
    parts = refs[:count]
    r1_ref, r2_ref, w_ref, acc_ref, normed_ref, scale_ref, out_ref = refs[count:]
    rows, cols, _ = out_ref.shape
    pitch = pad_to(cols, 16)
    total = parts[0][...]
    for s in range(1, count):
        total = total + parts[s][...].astype(F32)
    grad_right = total.astype(BF16).astype(F32)
    hidden = total.shape[1]
    grad = acc_ref[...] + matmul_t((grad_right * r1_ref[...]).astype(BF16), w_ref[:, 2 * hidden : 3 * hidden])
    grad = grad + matmul_t((grad_right * r2_ref[...]).astype(BF16), w_ref[:, 3 * hidden :])
    result = norm_back(grad, normed_ref[...], scale_ref[...]).astype(BF16)
    for i in range(rows):
        out_ref[i] = result[i * pitch : i * pitch + cols]


VMEM = pl.BlockSpec(memory_space=pltpu.VMEM)
HBM = pl.BlockSpec(memory_space=pltpu.HBM)


def call(body, outs, args, scratch=(), specs=VMEM, flops=10**7):
    outs = [jax.ShapeDtypeStruct(shape, dtype) for shape, dtype in outs]
    moved = sum(a.size * a.dtype.itemsize for a in [*args, *outs])
    scratch = [pltpu.VMEM(shape, F32) if isinstance(shape, tuple) else shape for shape in scratch]
    return pl.pallas_call(
        body,
        out_shape=outs,
        in_specs=[specs] * len(args),
        out_specs=[VMEM] * len(outs),
        scratch_shapes=scratch,
        compiler_params=pltpu.CompilerParams(vmem_limit_bytes=20 << 20),
        cost_estimate=pl.CostEstimate(flops=flops, bytes_accessed=moved, transcendentals=0),
    )(*args)


def on_device(devices, blocks, x, mask, w_proj, w_gate, w_out, cot):
    rows, cols, channels = x.shape
    hidden = w_out.shape[0]
    pitch, half, tall = pad_to(cols, 16), pad_to(rows, 16), pad_to(2 * rows, 16)
    cells, wide, mids = rows * pitch, 2 * rows * pitch, 2 * rows * half
    if devices != 2 * blocks or cols != 2 * rows or blocks & (blocks - 1) or rows % JB:
        raise ValueError("unsupported split")

    def along_dap(value, pairs):
        return lax.ppermute(value, "dap", [(2 * a + c, 2 * b + c) for a, b in pairs for c in range(2)])

    def along_ch(value, t):
        return lax.ppermute(value, "ch", [(h, h ^ t) for h in range(blocks)])

    def to_partner(value):
        return lax.ppermute(value, "dap", [(d, d ^ 1) for d in range(devices)])

    moves, shards = gather_plan(blocks)
    moved = []
    for pairs, source in moves:
        moved.append(along_dap(x if source is None else moved[source], pairs))
    x_pair, cot_pair = to_partner(x), to_partner(cot)
    sources = (x, cot, w_proj, w_gate, w_out)
    residues = mask.shape[0]
    xv, cotv, w_proj, w_gate, w_out, live = call(
        load_kernel,
        [(a.shape, a.dtype) for a in sources] + [((pad_to(residues + pitch - cols, 8), channels), F32)],
        [pltpu.with_memory_space_constraint(a, pltpu.HBM) for a in (mask, *sources)], [pltpu.SemaphoreType.DMA((6,)), pltpu.SMEM((residues,), jnp.int32)], specs=HBM)
    left, left_t, gate, upstream = call(
        left_kernel,
        [((wide, hidden), F32), ((cols * tall, hidden), F32), ((mids, channels), F32), ((mids, channels), F32)],
        (live, xv, x_pair, cotv, cot_pair, w_proj, w_gate),
        [(wide, channels), (tall * pitch, hidden), (wide, channels)])
    scratch = [(cells, channels), (cells, hidden), (tall * half, hidden)]
    steps = [[0] * blocks] + [table for _, table in shards]
    held = [[xv]] + [[moved[n] for n in group] for group, _ in shards]
    rights, done = [], []
    for s in range(blocks - 1):
        right, part = call(
            functools.partial(part_kernel, steps[s]), [((cells, hidden), BF16), ((mids, hidden), BF16)],
            (live, left_t, w_proj, *held[s]), scratch)
        rights.append(right)
        done.append(part)
    right, *parts = call(
        functools.partial(late_kernel, steps), [((cells, hidden), BF16)] + [((mids, hidden), BF16)] * blocks,
        (live, left_t, w_proj, *done, *held[-1]), scratch + [pltpu.VMEM((blocks, mids, hidden), BF16)])
    rights.append(right)
    for t in range(1, blocks):
        parts[t] = along_ch(parts[t], t)
    update, back, logit, grad_product = call(
        functools.partial(middle_kernel, blocks),
        [((mids // 2, channels), BF16), ((mids, channels), BF16), ((mids // 2, channels), BF16), ((mids, hidden), BF16)],
        (*parts, gate, upstream, w_out))
    pieces = [grad_product] + [along_ch(grad_product, t) for t in range(1, blocks)]
    back = to_partner(back)
    sends, returns, arrivals = reduce_plan(blocks)
    got = []
    for n, (table, extra) in enumerate(sends):
        more = () if extra is None else (got[extra],)
        (send,) = call(functools.partial(send_right_kernel, rows, cols, blocks, table),
                       [((cells, hidden), BF16)], (left, *pieces, *more), [(mids, hidden)])
        got += [along_dap(send, pairs) for pairs in returns[n]]
    left_own, left_send, right_own = call(
        functools.partial(grad_left_kernel, rows, cols, steps),
        [((cells, hidden), F32), ((cells, hidden), BF16), ((cells, hidden), F32)],
        (left, *pieces, *rights), [(blocks, mids, hidden), (blocks, cells, hidden)])
    left_got = to_partner(left_send)
    normed, scale, l1, l2, r1, r2 = call(
        factor_kernel, [((cells, hidden), F32)] * 6, (live, xv, w_proj),
        [(cells, channels)])
    pair_update, acc = call(
        finish_left_kernel, [((rows, cols, channels), BF16), ((cells, channels), F32)],
        (left_own, left_got, l1, l2, w_proj, w_gate, update, logit, back),
        [(cells, channels), (cells, channels)])
    (grad_pair,) = call(functools.partial(finish_kernel, 1 + len(arrivals)), [((rows, cols, channels), BF16)],
                        (right_own, *[got[n] for n in arrivals], r1, r2, w_proj, acc, normed, scale))
    return pair_update, grad_pair


def gather_plan(blocks):
    if blocks == 4:
        moves = [
            ([(0, 2), (3, 1), (1, 0), (2, 3)], None),
            ([(0, 1), (1, 3), (3, 2), (2, 0)], None),
            ([(1, 2), (2, 1)], None),
            ([(2, 3), (1, 0)], 0),
        ]
        return moves, [([0], [1, 2, 2, 1]), ([1], [2, 1, 1, 2]), ([2, 3], [3] * 4)]
    order = [*range(2, blocks, 2), 1, *range(3, blocks, 2)]
    moves = []
    for s in order:
        relay = s % 2 and s > 1
        moves.append(([(z, z ^ (1 if relay else s)) for z in range(blocks)], order.index(s ^ 1) if relay else None))
    return moves, [([n], [s] * blocks) for n, s in enumerate(order)]


def reduce_plan(blocks):
    if blocks == 4:
        sends = [([3] * 4, None), ([2, 1, 1, 2], None), ([1, 2, 2, 1], 0)]
        returns = [
            [[(3, 2), (0, 1)], [(1, 2), (2, 1)]],
            [[(1, 0), (3, 1), (2, 3), (0, 2)]],
            [[(2, 0), (1, 3), (0, 1), (3, 2)]],
        ]
        return sends, returns, [1, 2, 3]
    far = [*range(2, blocks), 1]
    sends = [([s] * blocks, None) for s in far]
    return sends, [[[(z, z ^ s) for z in range(blocks)]] for s in far], [*range(blocks - 1)]


def solution(mesh):
    blocks = mesh.shape["ch"]

    def body(*args):
        return on_device(mesh.shape["dap"], blocks, *args)

    return jax.shard_map(
        body,
        mesh=mesh,
        in_specs=(P("dap", "ch", None), P(), P(), P(), P(), P("dap", "ch", None)),
        out_specs=(P("dap", "ch", None), P("dap", "ch", None)),
        check_vma=False,
    )
```

```python
import functools

import jax
import jax.numpy as jnp
from jax import lax
from jax.experimental import pallas as pl
from jax.experimental.pallas import tpu as pltpu
from jax.sharding import PartitionSpec as P


EPSILON = 1e-05
F32 = jnp.float32
BF16 = jnp.bfloat16
JB = 5


def pad_to(count, tile):
    return (count + tile - 1) // tile * tile


def normalize(values):
    center = jnp.mean(values, axis=-1, keepdims=True)
    spread = values - center
    scale = lax.rsqrt(jnp.mean(spread * spread, axis=-1, keepdims=True) + EPSILON)
    return spread * scale, scale


def norm_back(grad, normed, scale):
    first = jnp.mean(grad, axis=-1, keepdims=True)
    second = jnp.mean(grad * normed, axis=-1, keepdims=True)
    return scale * (grad - first - normed * second)


def matmul(a, b):
    return lax.dot_general(a, b, (((1,), (0,)), ((), ())), preferred_element_type=F32)


def matmul_t(a, b):
    return lax.dot_general(a, b, (((1,), (1,)), ((), ())), preferred_element_type=F32)


def load_kernel(*refs):
    count = len(refs) // 2 - 1
    sources, outs, (sems, flags) = refs[:count], refs[count : 2 * count], refs[2 * count :]
    live_ref = outs[-1]
    copies = [pltpu.make_async_copy(sources[0], flags, sems.at[0])]
    copies += [pltpu.make_async_copy(a, b, sems.at[n + 1]) for n, (a, b) in enumerate(zip(sources[1:], outs[:-1]))]
    for copy in copies:
        copy.start()
    copies[0].wait()
    residues, total = flags.shape[0], live_ref.shape[0]
    for r in range(residues):
        live_ref[r : r + 1, :] = jnp.full((1, live_ref.shape[1]), flags[r].astype(F32))
    live_ref[residues:, :] = jnp.zeros((total - residues, live_ref.shape[1]), F32)
    for copy in copies[1:]:
        copy.wait()


def live_rows(live_ref, start, first, rows, pitch):
    columns = tiles(live_ref[pl.ds(first, pitch), :])
    for i in range(rows):
        yield i, (columns * row_of(live_ref, start + i)[None]).reshape(pitch, columns.shape[2])


def load_cells(cells_refs, scratch, first):
    rows, cols, channels = cells_refs[0].shape
    pitch = pad_to(cols, 16)
    for i in range(rows):
        at = (first + i) * pitch
        scratch[at : at + cols, :] = sum(ref[i].astype(F32) for ref in cells_refs)
        if pitch > cols:
            scratch[at + cols : at + pitch, :] = jnp.zeros((pitch - cols, channels), F32)


def row_of(ref, row):
    return ref[pl.ds(row, 8, stride=0), :]


def tiles(value):
    return value.reshape(value.shape[0] // 8, 8, value.shape[1])


def left_kernel(live_ref, x_ref, xp_ref, cot_ref, cotp_ref, w_ref, wg_ref,
                l_ref, lt_ref, gate_ref, cotm_ref, xs, ls, gs):
    rows, cols, channels = x_ref.shape
    pitch = pad_to(cols, 16)
    half = pad_to(rows, 16)
    hidden = w_ref.shape[1] // 4
    dap = lax.axis_index("dap")
    core = lax.rem(dap, 2)
    load_cells([x_ref], xs, 0)
    load_cells([xp_ref], xs, rows)
    normed, _ = normalize(xs[...])
    normed_half = normed.astype(BF16)
    projected = matmul(normed_half, w_ref[:, : 2 * hidden])
    left = jax.nn.sigmoid(projected[:, :hidden]) * projected[:, hidden:]
    for part, owner in enumerate((dap, dap + 1 - 2 * core)):
        for i, live in live_rows(live_ref, owner * rows, lax.axis_index("ch") * cols, rows, pitch):
            block = slice((part * rows + i) * pitch, (part * rows + i + 1) * pitch)
            value = (left[block] * live).astype(BF16).astype(F32)
            l_ref[block, :] = value
            ls[block, :] = value
    tall = pad_to(2 * rows, 16)
    ls[2 * rows * pitch :, :] = jnp.zeros(((tall - 2 * rows) * pitch, hidden), F32)
    for k in range(cols):
        lt_ref[k * tall : (k + 1) * tall, :] = ls[pl.ds(k, tall, stride=pitch), :]
    gs[...] = jax.nn.sigmoid(matmul(normed_half, wg_ref[...]))

    def pick(out_ref):
        for i in range(2 * rows):
            low = gs[i * pitch : i * pitch + rows, :]
            high = gs[i * pitch + rows : i * pitch + 2 * rows, :]
            out_ref[i * half : i * half + rows, :] = jnp.where(core == 0, low, high)
            if half > rows:
                out_ref[i * half + rows : (i + 1) * half, :] = jnp.zeros((half - rows, channels), F32)

    pick(gate_ref)
    load_cells([cot_ref], gs, 0)
    load_cells([cotp_ref], gs, rows)
    pick(cotm_ref)


def factor_kernel(live_ref, x_ref, w_ref, normed_ref, scale_ref, l1_ref, l2_ref, r1_ref, r2_ref, xs):
    rows, cols, _ = x_ref.shape
    pitch = pad_to(cols, 16)
    hidden = w_ref.shape[1] // 4
    load_cells([x_ref], xs, 0)
    normed, scale = normalize(xs[...])
    normed_ref[...] = normed
    scale_ref[...] = jnp.broadcast_to(scale, normed.shape)
    projected = matmul(normed.astype(BF16), w_ref[...])
    left_sig = jax.nn.sigmoid(projected[:, :hidden])
    right_sig = jax.nn.sigmoid(projected[:, 2 * hidden : 3 * hidden])
    left_in = projected[:, hidden : 2 * hidden] * left_sig * (1.0 - left_sig)
    right_in = projected[:, 3 * hidden :] * right_sig * (1.0 - right_sig)
    start = lax.axis_index("dap") * rows
    for i, live in live_rows(live_ref, start, lax.axis_index("ch") * cols, rows, pitch):
        block = slice(i * pitch, (i + 1) * pitch)
        l1_ref[block, :] = left_in[block] * live
        l2_ref[block, :] = left_sig[block] * live
        r1_ref[block, :] = right_in[block] * live
        r2_ref[block, :] = right_sig[block] * live


def product_part(lt_ref, rs, out, rows, cols):
    pitch, half, tall = pad_to(cols, 16), pad_to(rows, 16), pad_to(2 * rows, 16)

    def step(b, _):
        sums = [jnp.zeros((tall // 8, 8, rs.shape[1]), F32) for _ in range(JB)]
        for k in range(cols):
            left = tiles(lt_ref[k * tall : (k + 1) * tall, :])
            for n in range(JB):
                sums[n] = sums[n] + left * row_of(rs, (b * JB + n) * pitch + k)[None]
        for n in range(JB):
            out[pl.ds(b * JB + n, tall, stride=half), :] = sums[n].reshape(tall, rs.shape[1])
        return 0

    lax.fori_loop(0, rows // JB, step, 0)


def lookup(table, chip):
    value = table[0]
    for z in range(1, len(table)):
        if table[z] != table[0]:
            value = jnp.where(chip == z, table[z], value)
    return value


def this_chip():
    return lax.axis_index("dap") // 2


def right_of(live_ref, x_refs, w_ref, xs, rs, r_ref, s):
    rows, cols, _ = x_refs[0].shape
    pitch = pad_to(cols, 16)
    hidden = w_ref.shape[1] // 4
    load_cells(x_refs, xs, 0)
    normed, _ = normalize(xs[...])
    projected = matmul(normed.astype(BF16), w_ref[:, 2 * hidden :])
    right = jax.nn.sigmoid(projected[:, :hidden]) * projected[:, hidden:]
    start = (lax.axis_index("dap") ^ (2 * s)) * rows
    for i, live in live_rows(live_ref, start, lax.axis_index("ch") * cols, rows, pitch):
        block = slice(i * pitch, (i + 1) * pitch)
        value = (right[block] * live).astype(BF16)
        r_ref[block, :] = value
        rs[block, :] = value.astype(F32)


def part_kernel(steps, live_ref, lt_ref, w_ref, *refs):
    shards, (right_ref, part_ref, xs, rs, ps) = refs[:-5], refs[-5:]
    rows, cols, _ = shards[0].shape
    right_of(live_ref, shards, w_ref, xs, rs, right_ref, lookup(steps, this_chip()))
    product_part(lt_ref, rs, ps, rows, cols)
    part_ref[...] = ps[: part_ref.shape[0], :].astype(BF16)


def late_kernel(steps, live_ref, lt_ref, w_ref, *refs):
    blocks = len(steps)
    done, refs = refs[: blocks - 1], refs[blocks - 1 :]
    split = len(refs) - blocks - 5
    shards, right_ref, outs, (xs, rs, ps, held) = refs[:split], refs[split], refs[split + 1 : -4], refs[-4:]
    rows, cols, _ = shards[0].shape
    chip = this_chip()
    for part, table in zip(done, steps):
        held[lookup(table, chip)] = part[...]
    last = lookup(steps[-1], chip)
    right_of(live_ref, shards, w_ref, xs, rs, right_ref, last)
    product_part(lt_ref, rs, ps, rows, cols)
    held[last] = ps[: held.shape[1], :].astype(BF16)
    turn = chip ^ lax.axis_index("ch")
    for t in range(blocks):
        outs[t][...] = held[turn ^ t]


def middle_kernel(blocks, *refs):
    parts = refs[:blocks]
    gate_ref, cot_ref, w_ref, upd_ref, back_ref, logit_ref, gp_ref = refs[blocks:]
    total = parts[0][...].astype(F32)
    for t in range(1, blocks):
        total = total + parts[t][...].astype(F32)
    product = total.astype(BF16).astype(F32)
    hidden_norm, hidden_scale = normalize(product)
    out = matmul(hidden_norm.astype(BF16), w_ref[...])
    gate, upstream = gate_ref[...], cot_ref[...]
    grad_out = (upstream * gate).astype(BF16)
    grad_hidden = matmul_t(grad_out, w_ref[...])
    gp_ref[...] = norm_back(grad_hidden, hidden_norm, hidden_scale).astype(BF16)
    update = (gate * out).astype(BF16)
    logit = (upstream * out * gate * (1.0 - gate)).astype(BF16)
    own = upd_ref.shape[0]
    upd_ref[...] = update[:own]
    logit_ref[...] = logit[:own]
    back_ref[:own, :] = update[own:]
    back_ref[own:, :] = logit[own:]


def grad_right_part(l_ref, piece, store, rows, cols):
    pitch, half = pad_to(cols, 16), pad_to(rows, 16)

    def step(b, _):
        sums = [jnp.zeros((pitch // 8, 8, l_ref.shape[1]), F32) for _ in range(JB)]
        for i in range(2 * rows):
            left = tiles(l_ref[i * pitch : (i + 1) * pitch, :])
            for n in range(JB):
                sums[n] = sums[n] + left * row_of(piece, i * half + b * JB + n)[None]
        for n in range(JB):
            at = pl.multiple_of((b * JB + n) * pitch, pitch)
            store(pl.ds(at, pitch), sums[n].reshape(pitch, l_ref.shape[1]))
        return 0

    lax.fori_loop(0, rows // JB, step, 0)


def send_right_kernel(rows, cols, blocks, steps, *refs):
    l_ref, pieces = refs[0], refs[1 : 1 + blocks]
    more, (out_ref, gs) = refs[1 + blocks : -2], refs[-2:]
    chip, column = this_chip(), lax.axis_index("ch")
    step = lookup(steps, chip)
    for t in range(blocks):
        @pl.when(chip ^ column ^ step == t)
        def _(t=t):
            gs[...] = pieces[t][...].astype(F32)

    def store(where, value):
        for ref in more:
            value = value + ref[where, :].astype(F32)
        out_ref[where, :] = value.astype(BF16)

    grad_right_part(l_ref, gs, store, rows, cols)


def grad_left_part(piece_of, shard_of, first, blocks, ref, rows, cols):
    pitch, half, channels = pad_to(cols, 16), pad_to(rows, 16), ref.shape[1]

    def step(b, _):
        def block_step(m, sums):
            piece, shard = piece_of.at[m], shard_of.at[m]
            sums = list(sums)
            for j in range(rows):
                right = tiles(shard[j * pitch : (j + 1) * pitch, :])
                for n in range(JB):
                    row = (first + b * JB + n) * half + j
                    sums[n] = sums[n] + right * row_of(piece, row)[None]
            return tuple(sums)

        zero = jnp.zeros((pitch // 8, 8, channels), F32)
        sums = lax.fori_loop(0, blocks, block_step, (zero,) * JB)
        for n in range(JB):
            at = pl.multiple_of((b * JB + n) * pitch, pitch)
            ref[pl.ds(at, pitch), :] = sums[n].reshape(pitch, channels).astype(ref.dtype)
        return 0

    lax.fori_loop(0, rows // JB, step, 0)


def pair_left_kernel(rows, cols, steps, *refs):
    blocks = len(steps)
    pieces, shards, (send_ref, gs, rs) = refs[:blocks], refs[blocks : 2 * blocks], refs[2 * blocks :]
    chip, column = this_chip(), lax.axis_index("ch")
    for t in range(blocks):
        gs[column ^ t] = pieces[t][...].astype(F32)
    for table, shard in zip(steps, shards):
        rs[chip ^ lookup(table, chip)] = shard[...].astype(F32)
    grad_left_part(gs, rs, rows, blocks, send_ref, rows, cols)


def own_kernel(rows, cols, blocks, l_ref, gs, rs, left_ref, right_ref):
    grad_left_part(gs, rs, 0, blocks, left_ref, rows, cols)

    def store(where, value):
        right_ref[where, :] = value

    grad_right_part(l_ref, gs.at[this_chip()], store, rows, cols)


def finish_left_kernel(own_ref, got_ref, l1_ref, l2_ref, w_ref, wg_ref, upd_ref, logit_ref, back_ref,
                       out_ref, acc_ref, us, gs):
    rows, cols, channels = out_ref.shape
    pitch, half = pad_to(cols, 16), pad_to(rows, 16)
    mine = lax.rem(lax.axis_index("dap"), 2) == 0
    for i in range(rows):
        for scratch, ref, base in ((us, upd_ref, 0), (gs, logit_ref, rows * half)):
            here = ref[i * half : (i + 1) * half, :].astype(F32)[:rows]
            there = back_ref[base + i * half : base + (i + 1) * half, :].astype(F32)[:rows]
            scratch[i * pitch : i * pitch + rows, :] = jnp.where(mine, here, there)
            scratch[i * pitch + rows : i * pitch + 2 * rows, :] = jnp.where(mine, there, here)
            if pitch > cols:
                scratch[i * pitch + cols : (i + 1) * pitch, :] = jnp.zeros((pitch - cols, channels), F32)
        out_ref[i] = us[i * pitch : i * pitch + cols, :].astype(BF16)
    grad_left = (own_ref[...] + got_ref[...].astype(F32)).astype(BF16).astype(F32)
    hidden = own_ref.shape[1]
    acc = matmul_t((grad_left * l1_ref[...]).astype(BF16), w_ref[:, :hidden])
    acc = acc + matmul_t((grad_left * l2_ref[...]).astype(BF16), w_ref[:, hidden : 2 * hidden])
    acc_ref[...] = acc + matmul_t(gs[...].astype(BF16), wg_ref[...])


def finish_kernel(count, *refs):
    parts = refs[:count]
    r1_ref, r2_ref, w_ref, acc_ref, normed_ref, scale_ref, out_ref = refs[count:]
    rows, cols, _ = out_ref.shape
    pitch = pad_to(cols, 16)
    total = parts[0][...]
    for s in range(1, count):
        total = total + parts[s][...].astype(F32)
    grad_right = total.astype(BF16).astype(F32)
    hidden = total.shape[1]
    grad = acc_ref[...] + matmul_t((grad_right * r1_ref[...]).astype(BF16), w_ref[:, 2 * hidden : 3 * hidden])
    grad = grad + matmul_t((grad_right * r2_ref[...]).astype(BF16), w_ref[:, 3 * hidden :])
    result = norm_back(grad, normed_ref[...], scale_ref[...]).astype(BF16)
    for i in range(rows):
        out_ref[i] = result[i * pitch : i * pitch + cols]


VMEM = pl.BlockSpec(memory_space=pltpu.VMEM)
HBM = pl.BlockSpec(memory_space=pltpu.HBM)


def call(body, outs, args, scratch=(), specs=VMEM, flops=10**7):
    outs = [jax.ShapeDtypeStruct(shape, dtype) for shape, dtype in outs]
    moved = sum(a.size * a.dtype.itemsize for a in [*args, *outs])
    scratch = [pltpu.VMEM(shape, F32) if isinstance(shape, tuple) else shape for shape in scratch]
    return pl.pallas_call(
        body,
        out_shape=outs,
        in_specs=[specs] * len(args),
        out_specs=[VMEM] * len(outs),
        scratch_shapes=scratch,
        compiler_params=pltpu.CompilerParams(vmem_limit_bytes=20 << 20),
        cost_estimate=pl.CostEstimate(flops=flops, bytes_accessed=moved, transcendentals=0),
    )(*args)


def on_device(devices, blocks, x, mask, w_proj, w_gate, w_out, cot):
    rows, cols, channels = x.shape
    hidden = w_out.shape[0]
    pitch, half, tall = pad_to(cols, 16), pad_to(rows, 16), pad_to(2 * rows, 16)
    cells, wide, mids = rows * pitch, 2 * rows * pitch, 2 * rows * half
    if devices != 2 * blocks or cols != 2 * rows or blocks & (blocks - 1) or rows % JB:
        raise ValueError("unsupported split")

    def along_dap(value, pairs):
        return lax.ppermute(value, "dap", [(2 * a + c, 2 * b + c) for a, b in pairs for c in range(2)])

    def along_ch(value, t):
        return lax.ppermute(value, "ch", [(h, h ^ t) for h in range(blocks)])

    def to_partner(value):
        return lax.ppermute(value, "dap", [(d, d ^ 1) for d in range(devices)])

    moves, shards = gather_plan(blocks)
    moved = []
    for pairs, source in moves:
        moved.append(along_dap(x if source is None else moved[source], pairs))
    x_pair, cot_pair = to_partner(x), to_partner(cot)
    sources = (x, cot, w_proj, w_gate, w_out)
    residues = mask.shape[0]
    xv, cotv, w_proj, w_gate, w_out, live = call(
        load_kernel,
        [(a.shape, a.dtype) for a in sources] + [((pad_to(residues + pitch - cols, 8), channels), F32)],
        [pltpu.with_memory_space_constraint(a, pltpu.HBM) for a in (mask, *sources)], [pltpu.SemaphoreType.DMA((6,)), pltpu.SMEM((residues,), jnp.int32)], specs=HBM)
    left, left_t, gate, upstream = call(
        left_kernel,
        [((wide, hidden), F32), ((cols * tall, hidden), F32), ((mids, channels), F32), ((mids, channels), F32)],
        (live, xv, x_pair, cotv, cot_pair, w_proj, w_gate),
        [(wide, channels), (tall * pitch, hidden), (wide, channels)])
    scratch = [(cells, channels), (cells, hidden), (tall * half, hidden)]
    steps = [[0] * blocks] + [table for _, table in shards]
    held = [[xv]] + [[moved[n] for n in group] for group, _ in shards]
    rights, done = [], []
    for s in range(blocks - 1):
        right, part = call(
            functools.partial(part_kernel, steps[s]), [((cells, hidden), BF16), ((mids, hidden), BF16)],
            (live, left_t, w_proj, *held[s]), scratch)
        rights.append(right)
        done.append(part)
    right, *parts = call(
        functools.partial(late_kernel, steps), [((cells, hidden), BF16)] + [((mids, hidden), BF16)] * blocks,
        (live, left_t, w_proj, *done, *held[-1]), scratch + [pltpu.VMEM((blocks, mids, hidden), BF16)])
    rights.append(right)
    for t in range(1, blocks):
        parts[t] = along_ch(parts[t], t)
    update, back, logit, grad_product = call(
        functools.partial(middle_kernel, blocks),
        [((mids // 2, channels), BF16), ((mids, channels), BF16), ((mids // 2, channels), BF16), ((mids, hidden), BF16)],
        (*parts, gate, upstream, w_out))
    pieces = [grad_product] + [along_ch(grad_product, t) for t in range(1, blocks)]
    back = to_partner(back)
    sends, returns, arrivals = reduce_plan(blocks)
    got = []
    for n, (table, extra) in enumerate(sends):
        more = () if extra is None else (got[extra],)
        (send,) = call(functools.partial(send_right_kernel, rows, cols, blocks, table),
                       [((cells, hidden), BF16)], (left, *pieces, *more), [(mids, hidden)])
        got += [along_dap(send, pairs) for pairs in returns[n]]
    left_send, staged, rights_staged = call(
        functools.partial(pair_left_kernel, rows, cols, steps),
        [((cells, hidden), BF16), ((blocks, mids, hidden), F32), ((blocks, cells, hidden), F32)], (*pieces, *rights))
    left_got = to_partner(left_send)
    left_own, right_own = call(
        functools.partial(own_kernel, rows, cols, blocks), [((cells, hidden), F32)] * 2,
        (left, staged, rights_staged))
    normed, scale, l1, l2, r1, r2 = call(
        factor_kernel, [((cells, hidden), F32)] * 6, (live, xv, w_proj),
        [(cells, channels)])
    pair_update, acc = call(
        finish_left_kernel, [((rows, cols, channels), BF16), ((cells, channels), F32)],
        (left_own, left_got, l1, l2, w_proj, w_gate, update, logit, back),
        [(cells, channels), (cells, channels)])
    (grad_pair,) = call(functools.partial(finish_kernel, 1 + len(arrivals)), [((rows, cols, channels), BF16)],
                        (right_own, *[got[n] for n in arrivals], r1, r2, w_proj, acc, normed, scale))
    return pair_update, grad_pair


def gather_plan(blocks):
    order = [*range(2, blocks, 2), 1, *range(3, blocks, 2)]
    moves = []
    for s in order:
        relay = s % 2 and s > 1
        moves.append(([(z, z ^ (1 if relay else s)) for z in range(blocks)], order.index(s ^ 1) if relay else None))
    return moves, [([n], [s] * blocks) for n, s in enumerate(order)]


def reduce_plan(blocks):
    far = [*range(2, blocks), 1]
    sends = [([s] * blocks, None) for s in far]
    return sends, [[[(z, z ^ s) for z in range(blocks)]] for s in far], [*range(blocks - 1)]


def solution(mesh):
    blocks = mesh.shape["ch"]

    def body(*args):
        return on_device(mesh.shape["dap"], blocks, *args)

    return jax.shard_map(
        body,
        mesh=mesh,
        in_specs=(P("dap", "ch", None), P(), P(), P(), P(), P("dap", "ch", None)),
        out_specs=(P("dap", "ch", None), P("dap", "ch", None)),
        check_vma=False,
    )
```

```python
import functools

import jax
import jax.numpy as jnp
from jax import lax
from jax.experimental import pallas as pl
from jax.experimental.pallas import tpu as pltpu
from jax.sharding import PartitionSpec as P


EPSILON = 1e-05
F32 = jnp.float32
BF16 = jnp.bfloat16
JB = 5


def pad_to(count, tile):
    return (count + tile - 1) // tile * tile


def normalize(values):
    center = jnp.mean(values, axis=-1, keepdims=True)
    spread = values - center
    scale = lax.rsqrt(jnp.mean(spread * spread, axis=-1, keepdims=True) + EPSILON)
    return spread * scale, scale


def norm_back(grad, normed, scale):
    first = jnp.mean(grad, axis=-1, keepdims=True)
    second = jnp.mean(grad * normed, axis=-1, keepdims=True)
    return scale * (grad - first - normed * second)


def matmul(a, b):
    return lax.dot_general(a, b, (((1,), (0,)), ((), ())), preferred_element_type=F32)


def matmul_t(a, b):
    return lax.dot_general(a, b, (((1,), (1,)), ((), ())), preferred_element_type=F32)


def load_kernel(*refs):
    count = len(refs) // 2 - 1
    sources, outs, (sems, flags) = refs[:count], refs[count : 2 * count], refs[2 * count :]
    live_ref = outs[-1]
    copies = [pltpu.make_async_copy(sources[0], flags, sems.at[0])]
    copies += [pltpu.make_async_copy(a, b, sems.at[n + 1]) for n, (a, b) in enumerate(zip(sources[1:], outs[:-1]))]
    for copy in copies:
        copy.start()
    copies[0].wait()
    residues, total = flags.shape[0], live_ref.shape[0]
    for r in range(residues):
        live_ref[r : r + 1, :] = jnp.full((1, live_ref.shape[1]), flags[r].astype(F32))
    live_ref[residues:, :] = jnp.zeros((total - residues, live_ref.shape[1]), F32)
    for copy in copies[1:]:
        copy.wait()


def live_rows(live_ref, start, first, rows, pitch):
    columns = tiles(live_ref[pl.ds(first, pitch), :])
    for i in range(rows):
        yield i, (columns * row_of(live_ref, start + i)[None]).reshape(pitch, columns.shape[2])


def load_cells(cells_refs, scratch, first):
    rows, cols, channels = cells_refs[0].shape
    pitch = pad_to(cols, 16)
    for i in range(rows):
        at = (first + i) * pitch
        scratch[at : at + cols, :] = sum(ref[i].astype(F32) for ref in cells_refs)
        if pitch > cols:
            scratch[at + cols : at + pitch, :] = jnp.zeros((pitch - cols, channels), F32)


def row_of(ref, row):
    return ref[pl.ds(row, 8, stride=0), :]


def tiles(value):
    return value.reshape(value.shape[0] // 8, 8, value.shape[1])


def left_kernel(live_ref, x_ref, xp_ref, cot_ref, cotp_ref, w_ref, wg_ref,
                l_ref, lt_ref, gate_ref, cotm_ref, xs, ls, gs):
    rows, cols, channels = x_ref.shape
    pitch = pad_to(cols, 16)
    half = pad_to(rows, 16)
    hidden = w_ref.shape[1] // 4
    dap = lax.axis_index("dap")
    core = lax.rem(dap, 2)
    load_cells([x_ref], xs, 0)
    load_cells([xp_ref], xs, rows)
    normed, _ = normalize(xs[...])
    normed_half = normed.astype(BF16)
    projected = matmul(normed_half, w_ref[:, : 2 * hidden])
    left = jax.nn.sigmoid(projected[:, :hidden]) * projected[:, hidden:]
    for part, owner in enumerate((dap, dap + 1 - 2 * core)):
        for i, live in live_rows(live_ref, owner * rows, lax.axis_index("ch") * cols, rows, pitch):
            block = slice((part * rows + i) * pitch, (part * rows + i + 1) * pitch)
            value = (left[block] * live).astype(BF16).astype(F32)
            l_ref[block, :] = value
            ls[block, :] = value
    tall = pad_to(2 * rows, 16)
    ls[2 * rows * pitch :, :] = jnp.zeros(((tall - 2 * rows) * pitch, hidden), F32)
    for k in range(cols):
        lt_ref[k * tall : (k + 1) * tall, :] = ls[pl.ds(k, tall, stride=pitch), :]
    gs[...] = jax.nn.sigmoid(matmul(normed_half, wg_ref[...]))

    def pick(out_ref):
        for i in range(2 * rows):
            low = gs[i * pitch : i * pitch + rows, :]
            high = gs[i * pitch + rows : i * pitch + 2 * rows, :]
            out_ref[i * half : i * half + rows, :] = jnp.where(core == 0, low, high)
            if half > rows:
                out_ref[i * half + rows : (i + 1) * half, :] = jnp.zeros((half - rows, channels), F32)

    pick(gate_ref)
    load_cells([cot_ref], gs, 0)
    load_cells([cotp_ref], gs, rows)
    pick(cotm_ref)


def factor_kernel(live_ref, x_ref, w_ref, normed_ref, scale_ref, l1_ref, l2_ref, r1_ref, r2_ref, xs):
    rows, cols, _ = x_ref.shape
    pitch = pad_to(cols, 16)
    hidden = w_ref.shape[1] // 4
    load_cells([x_ref], xs, 0)
    normed, scale = normalize(xs[...])
    normed_ref[...] = normed
    scale_ref[...] = jnp.broadcast_to(scale, normed.shape)
    projected = matmul(normed.astype(BF16), w_ref[...])
    left_sig = jax.nn.sigmoid(projected[:, :hidden])
    right_sig = jax.nn.sigmoid(projected[:, 2 * hidden : 3 * hidden])
    left_in = projected[:, hidden : 2 * hidden] * left_sig * (1.0 - left_sig)
    right_in = projected[:, 3 * hidden :] * right_sig * (1.0 - right_sig)
    start = lax.axis_index("dap") * rows
    for i, live in live_rows(live_ref, start, lax.axis_index("ch") * cols, rows, pitch):
        block = slice(i * pitch, (i + 1) * pitch)
        l1_ref[block, :] = left_in[block] * live
        l2_ref[block, :] = left_sig[block] * live
        r1_ref[block, :] = right_in[block] * live
        r2_ref[block, :] = right_sig[block] * live


def product_part(lt_ref, rs, out, rows, cols):
    pitch, half, tall = pad_to(cols, 16), pad_to(rows, 16), pad_to(2 * rows, 16)

    def step(b, _):
        sums = [jnp.zeros((tall // 8, 8, rs.shape[1]), F32) for _ in range(JB)]
        for k in range(cols):
            left = tiles(lt_ref[k * tall : (k + 1) * tall, :])
            for n in range(JB):
                sums[n] = sums[n] + left * row_of(rs, (b * JB + n) * pitch + k)[None]
        for n in range(JB):
            out[pl.ds(b * JB + n, tall, stride=half), :] = sums[n].reshape(tall, rs.shape[1])
        return 0

    lax.fori_loop(0, rows // JB, step, 0)


def lookup(table, chip):
    value = table[0]
    for z in range(1, len(table)):
        if table[z] != table[0]:
            value = jnp.where(chip == z, table[z], value)
    return value


def turn_of(n, blocks, core):
    return n if core == 0 or n == 0 else blocks - n


def my_turn(n, blocks):
    return jnp.where(lax.axis_index("dap") % 2 == 0, turn_of(n, blocks, 0), turn_of(n, blocks, 1))


def this_chip():
    return lax.axis_index("dap") // 2


def right_of(live_ref, x_refs, w_ref, xs, rs, r_ref, s):
    rows, cols, _ = x_refs[0].shape
    pitch = pad_to(cols, 16)
    hidden = w_ref.shape[1] // 4
    load_cells(x_refs, xs, 0)
    normed, _ = normalize(xs[...])
    projected = matmul(normed.astype(BF16), w_ref[:, 2 * hidden :])
    right = jax.nn.sigmoid(projected[:, :hidden]) * projected[:, hidden:]
    start = (lax.axis_index("dap") ^ (2 * s)) * rows
    for i, live in live_rows(live_ref, start, lax.axis_index("ch") * cols, rows, pitch):
        block = slice(i * pitch, (i + 1) * pitch)
        value = (right[block] * live).astype(BF16)
        r_ref[block, :] = value
        rs[block, :] = value.astype(F32)


def part_kernel(steps, live_ref, lt_ref, w_ref, *refs):
    shards, (right_ref, part_ref, xs, rs, ps) = refs[:-5], refs[-5:]
    rows, cols, _ = shards[0].shape
    right_of(live_ref, shards, w_ref, xs, rs, right_ref, lookup(steps, this_chip()))
    product_part(lt_ref, rs, ps, rows, cols)
    part_ref[...] = ps[: part_ref.shape[0], :].astype(BF16)


def late_kernel(steps, live_ref, lt_ref, w_ref, *refs):
    blocks = len(steps)
    done, refs = refs[: blocks - 1], refs[blocks - 1 :]
    split = len(refs) - blocks - 5
    shards, right_ref, outs, (xs, rs, ps, held) = refs[:split], refs[split], refs[split + 1 : -4], refs[-4:]
    rows, cols, _ = shards[0].shape
    chip = this_chip()
    for part, table in zip(done, steps):
        held[lookup(table, chip)] = part[...]
    last = lookup(steps[-1], chip)
    right_of(live_ref, shards, w_ref, xs, rs, right_ref, last)
    product_part(lt_ref, rs, ps, rows, cols)
    held[last] = ps[: held.shape[1], :].astype(BF16)
    turn = chip ^ lax.axis_index("ch")
    for t in range(blocks):
        outs[t][...] = held[turn ^ my_turn(t, blocks)]


def middle_kernel(blocks, *refs):
    parts = refs[:blocks]
    gate_ref, cot_ref, w_ref, upd_ref, back_ref, logit_ref, gp_ref = refs[blocks:]
    total = parts[0][...].astype(F32)
    for t in range(1, blocks):
        total = total + parts[t][...].astype(F32)
    product = total.astype(BF16).astype(F32)
    hidden_norm, hidden_scale = normalize(product)
    out = matmul(hidden_norm.astype(BF16), w_ref[...])
    gate, upstream = gate_ref[...], cot_ref[...]
    grad_out = (upstream * gate).astype(BF16)
    grad_hidden = matmul_t(grad_out, w_ref[...])
    gp_ref[...] = norm_back(grad_hidden, hidden_norm, hidden_scale).astype(BF16)
    update = (gate * out).astype(BF16)
    logit = (upstream * out * gate * (1.0 - gate)).astype(BF16)
    own = upd_ref.shape[0]
    upd_ref[...] = update[:own]
    logit_ref[...] = logit[:own]
    back_ref[:own, :] = update[own:]
    back_ref[own:, :] = logit[own:]


def grad_right_part(l_ref, piece, store, rows, cols):
    pitch, half = pad_to(cols, 16), pad_to(rows, 16)

    def step(b, _):
        sums = [jnp.zeros((pitch // 8, 8, l_ref.shape[1]), F32) for _ in range(JB)]
        for i in range(2 * rows):
            left = tiles(l_ref[i * pitch : (i + 1) * pitch, :])
            for n in range(JB):
                sums[n] = sums[n] + left * row_of(piece, i * half + b * JB + n)[None]
        for n in range(JB):
            at = pl.multiple_of((b * JB + n) * pitch, pitch)
            store(pl.ds(at, pitch), sums[n].reshape(pitch, l_ref.shape[1]))
        return 0

    lax.fori_loop(0, rows // JB, step, 0)


def send_right_kernel(rows, cols, blocks, steps, *refs):
    l_ref, pieces = refs[0], refs[1 : 1 + blocks]
    more, (out_ref, gs) = refs[1 + blocks : -2], refs[-2:]
    chip, column = this_chip(), lax.axis_index("ch")
    step = lookup(steps, chip)
    for t in range(blocks):
        @pl.when(chip ^ column ^ step == my_turn(t, blocks))
        def _(t=t):
            gs[...] = pieces[t][...].astype(F32)

    def store(where, value):
        for ref in more:
            value = value + ref[where, :].astype(F32)
        out_ref[where, :] = value.astype(BF16)

    grad_right_part(l_ref, gs, store, rows, cols)


def grad_left_part(piece_of, shard_of, first, blocks, ref, rows, cols):
    pitch, half, channels = pad_to(cols, 16), pad_to(rows, 16), ref.shape[1]

    def step(b, _):
        def block_step(m, sums):
            piece, shard = piece_of.at[m], shard_of.at[m]
            sums = list(sums)
            for j in range(rows):
                right = tiles(shard[j * pitch : (j + 1) * pitch, :])
                for n in range(JB):
                    row = (first + b * JB + n) * half + j
                    sums[n] = sums[n] + right * row_of(piece, row)[None]
            return tuple(sums)

        zero = jnp.zeros((pitch // 8, 8, channels), F32)
        sums = lax.fori_loop(0, blocks, block_step, (zero,) * JB)
        for n in range(JB):
            at = pl.multiple_of((b * JB + n) * pitch, pitch)
            ref[pl.ds(at, pitch), :] = sums[n].reshape(pitch, channels).astype(ref.dtype)
        return 0

    lax.fori_loop(0, rows // JB, step, 0)


def pair_left_kernel(rows, cols, steps, *refs):
    blocks = len(steps)
    pieces, shards, (send_ref, gs, rs) = refs[:blocks], refs[blocks : 2 * blocks], refs[2 * blocks :]
    chip, column = this_chip(), lax.axis_index("ch")
    for t in range(blocks):
        gs[column ^ my_turn(t, blocks)] = pieces[t][...].astype(F32)
    for table, shard in zip(steps, shards):
        rs[chip ^ lookup(table, chip)] = shard[...].astype(F32)
    grad_left_part(gs, rs, rows, blocks, send_ref, rows, cols)


def own_kernel(rows, cols, blocks, l_ref, gs, rs, left_ref, right_ref):
    grad_left_part(gs, rs, 0, blocks, left_ref, rows, cols)

    def store(where, value):
        right_ref[where, :] = value

    grad_right_part(l_ref, gs.at[this_chip()], store, rows, cols)


def finish_left_kernel(own_ref, got_ref, l1_ref, l2_ref, w_ref, wg_ref, upd_ref, logit_ref, back_ref,
                       out_ref, acc_ref, us, gs):
    rows, cols, channels = out_ref.shape
    pitch, half = pad_to(cols, 16), pad_to(rows, 16)
    mine = lax.rem(lax.axis_index("dap"), 2) == 0
    for i in range(rows):
        for scratch, ref, base in ((us, upd_ref, 0), (gs, logit_ref, rows * half)):
            here = ref[i * half : (i + 1) * half, :].astype(F32)[:rows]
            there = back_ref[base + i * half : base + (i + 1) * half, :].astype(F32)[:rows]
            scratch[i * pitch : i * pitch + rows, :] = jnp.where(mine, here, there)
            scratch[i * pitch + rows : i * pitch + 2 * rows, :] = jnp.where(mine, there, here)
            if pitch > cols:
                scratch[i * pitch + cols : (i + 1) * pitch, :] = jnp.zeros((pitch - cols, channels), F32)
        out_ref[i] = us[i * pitch : i * pitch + cols, :].astype(BF16)
    grad_left = (own_ref[...] + got_ref[...].astype(F32)).astype(BF16).astype(F32)
    hidden = own_ref.shape[1]
    acc = matmul_t((grad_left * l1_ref[...]).astype(BF16), w_ref[:, :hidden])
    acc = acc + matmul_t((grad_left * l2_ref[...]).astype(BF16), w_ref[:, hidden : 2 * hidden])
    acc_ref[...] = acc + matmul_t(gs[...].astype(BF16), wg_ref[...])


def finish_kernel(count, *refs):
    parts = refs[:count]
    r1_ref, r2_ref, w_ref, acc_ref, normed_ref, scale_ref, out_ref = refs[count:]
    rows, cols, _ = out_ref.shape
    pitch = pad_to(cols, 16)
    total = parts[0][...]
    for s in range(1, count):
        total = total + parts[s][...].astype(F32)
    grad_right = total.astype(BF16).astype(F32)
    hidden = total.shape[1]
    grad = acc_ref[...] + matmul_t((grad_right * r1_ref[...]).astype(BF16), w_ref[:, 2 * hidden : 3 * hidden])
    grad = grad + matmul_t((grad_right * r2_ref[...]).astype(BF16), w_ref[:, 3 * hidden :])
    result = norm_back(grad, normed_ref[...], scale_ref[...]).astype(BF16)
    for i in range(rows):
        out_ref[i] = result[i * pitch : i * pitch + cols]


VMEM = pl.BlockSpec(memory_space=pltpu.VMEM)
HBM = pl.BlockSpec(memory_space=pltpu.HBM)


def call(body, outs, args, scratch=(), specs=VMEM, flops=10**7):
    outs = [jax.ShapeDtypeStruct(shape, dtype) for shape, dtype in outs]
    moved = sum(a.size * a.dtype.itemsize for a in [*args, *outs])
    scratch = [pltpu.VMEM(shape, F32) if isinstance(shape, tuple) else shape for shape in scratch]
    return pl.pallas_call(
        body,
        out_shape=outs,
        in_specs=[specs] * len(args),
        out_specs=[VMEM] * len(outs),
        scratch_shapes=scratch,
        compiler_params=pltpu.CompilerParams(vmem_limit_bytes=20 << 20),
        cost_estimate=pl.CostEstimate(flops=flops, bytes_accessed=moved, transcendentals=0),
    )(*args)


def on_device(devices, blocks, x, mask, w_proj, w_gate, w_out, cot):
    rows, cols, channels = x.shape
    hidden = w_out.shape[0]
    pitch, half, tall = pad_to(cols, 16), pad_to(rows, 16), pad_to(2 * rows, 16)
    cells, wide, mids = rows * pitch, 2 * rows * pitch, 2 * rows * half
    if devices != 2 * blocks or cols != 2 * rows or blocks & (blocks - 1) or rows % JB:
        raise ValueError("unsupported split")

    def along_dap(value, pairs):
        return lax.ppermute(value, "dap", [(2 * a + c, 2 * b + c) for a, b in pairs for c in range(2)])

    def along_ch(value, t):
        return lax.ppermute(value, ("dap", "ch"), [
            (d * blocks + h, d * blocks + (h ^ turn_of(t, blocks, d % 2))) for d in range(devices) for h in range(blocks)])

    def to_partner(value):
        return lax.ppermute(value, "dap", [(d, d ^ 1) for d in range(devices)])

    moves, shards = gather_plan(blocks)
    moved = []
    for pairs, source in moves:
        moved.append(along_dap(x if source is None else moved[source], pairs))
    x_pair, cot_pair = to_partner(x), to_partner(cot)
    sources = (x, cot, w_proj, w_gate, w_out)
    residues = mask.shape[0]
    xv, cotv, w_proj, w_gate, w_out, live = call(
        load_kernel,
        [(a.shape, a.dtype) for a in sources] + [((pad_to(residues + pitch - cols, 8), channels), F32)],
        [pltpu.with_memory_space_constraint(a, pltpu.HBM) for a in (mask, *sources)], [pltpu.SemaphoreType.DMA((6,)), pltpu.SMEM((residues,), jnp.int32)], specs=HBM)
    left, left_t, gate, upstream = call(
        left_kernel,
        [((wide, hidden), F32), ((cols * tall, hidden), F32), ((mids, channels), F32), ((mids, channels), F32)],
        (live, xv, x_pair, cotv, cot_pair, w_proj, w_gate),
        [(wide, channels), (tall * pitch, hidden), (wide, channels)])
    scratch = [(cells, channels), (cells, hidden), (tall * half, hidden)]
    steps = [[0] * blocks] + [table for _, table in shards]
    held = [[xv]] + [[moved[n] for n in group] for group, _ in shards]
    rights, done = [], []
    for s in range(blocks - 1):
        right, part = call(
            functools.partial(part_kernel, steps[s]), [((cells, hidden), BF16), ((mids, hidden), BF16)],
            (live, left_t, w_proj, *held[s]), scratch)
        rights.append(right)
        done.append(part)
    right, *parts = call(
        functools.partial(late_kernel, steps), [((cells, hidden), BF16)] + [((mids, hidden), BF16)] * blocks,
        (live, left_t, w_proj, *done, *held[-1]), scratch + [pltpu.VMEM((blocks, mids, hidden), BF16)])
    rights.append(right)
    for t in range(1, blocks):
        parts[t] = along_ch(parts[t], t)
    update, back, logit, grad_product = call(
        functools.partial(middle_kernel, blocks),
        [((mids // 2, channels), BF16), ((mids, channels), BF16), ((mids // 2, channels), BF16), ((mids, hidden), BF16)],
        (*parts, gate, upstream, w_out))
    pieces = [grad_product] + [along_ch(grad_product, t) for t in range(1, blocks)]
    back = to_partner(back)
    sends, returns, arrivals = reduce_plan(blocks)
    got = []
    for n, (table, extra) in enumerate(sends):
        more = () if extra is None else (got[extra],)
        (send,) = call(functools.partial(send_right_kernel, rows, cols, blocks, table),
                       [((cells, hidden), BF16)], (left, *pieces, *more), [(mids, hidden)])
        got += [along_dap(send, pairs) for pairs in returns[n]]
    left_send, staged, rights_staged = call(
        functools.partial(pair_left_kernel, rows, cols, steps),
        [((cells, hidden), BF16), ((blocks, mids, hidden), F32), ((blocks, cells, hidden), F32)], (*pieces, *rights))
    left_got = to_partner(left_send)
    left_own, right_own = call(
        functools.partial(own_kernel, rows, cols, blocks), [((cells, hidden), F32)] * 2,
        (left, staged, rights_staged))
    normed, scale, l1, l2, r1, r2 = call(
        factor_kernel, [((cells, hidden), F32)] * 6, (live, xv, w_proj),
        [(cells, channels)])
    pair_update, acc = call(
        finish_left_kernel, [((rows, cols, channels), BF16), ((cells, channels), F32)],
        (left_own, left_got, l1, l2, w_proj, w_gate, update, logit, back),
        [(cells, channels), (cells, channels)])
    (grad_pair,) = call(functools.partial(finish_kernel, 1 + len(arrivals)), [((rows, cols, channels), BF16)],
                        (right_own, *[got[n] for n in arrivals], r1, r2, w_proj, acc, normed, scale))
    return pair_update, grad_pair


def gather_plan(blocks):
    order = [*range(2, blocks, 2), 1, *range(3, blocks, 2)]
    moves = []
    for s in order:
        relay = s % 2 and s > 1
        moves.append(([(z, z ^ (1 if relay else s)) for z in range(blocks)], order.index(s ^ 1) if relay else None))
    return moves, [([n], [s] * blocks) for n, s in enumerate(order)]


def reduce_plan(blocks):
    far = [*range(2, blocks), 1]
    sends = [([s] * blocks, None) for s in far]
    return sends, [[[(z, z ^ s) for z in range(blocks)]] for s in far], [*range(blocks - 1)]


def solution(mesh):
    blocks = mesh.shape["ch"]

    def body(*args):
        return on_device(mesh.shape["dap"], blocks, *args)

    return jax.shard_map(
        body,
        mesh=mesh,
        in_specs=(P("dap", "ch", None), P(), P(), P(), P(), P("dap", "ch", None)),
        out_specs=(P("dap", "ch", None), P("dap", "ch", None)),
        check_vma=False,
    )
```

```python
import functools

import jax
import jax.numpy as jnp
from jax import lax
from jax.experimental import pallas as pl
from jax.experimental.pallas import tpu as pltpu
from jax.sharding import PartitionSpec as P


EPSILON = 1e-05
F32 = jnp.float32
BF16 = jnp.bfloat16
JB = 5


def pad_to(count, tile):
    return (count + tile - 1) // tile * tile


def normalize(values):
    center = jnp.mean(values, axis=-1, keepdims=True)
    spread = values - center
    scale = lax.rsqrt(jnp.mean(spread * spread, axis=-1, keepdims=True) + EPSILON)
    return spread * scale, scale


def norm_back(grad, normed, scale):
    first = jnp.mean(grad, axis=-1, keepdims=True)
    second = jnp.mean(grad * normed, axis=-1, keepdims=True)
    return scale * (grad - first - normed * second)


def matmul(a, b):
    return lax.dot_general(a, b, (((1,), (0,)), ((), ())), preferred_element_type=F32)


def matmul_t(a, b):
    return lax.dot_general(a, b, (((1,), (1,)), ((), ())), preferred_element_type=F32)


def load_kernel(*refs):
    count = len(refs) // 2 - 1
    sources, outs, (sems, flags) = refs[:count], refs[count : 2 * count], refs[2 * count :]
    live_ref = outs[-1]
    copies = [pltpu.make_async_copy(sources[0], flags, sems.at[0])]
    copies += [pltpu.make_async_copy(a, b, sems.at[n + 1]) for n, (a, b) in enumerate(zip(sources[1:], outs[:-1]))]
    for copy in copies:
        copy.start()
    copies[0].wait()
    residues, total = flags.shape[0], live_ref.shape[0]
    for r in range(residues):
        live_ref[r : r + 1, :] = jnp.full((1, live_ref.shape[1]), flags[r].astype(F32))
    live_ref[residues:, :] = jnp.zeros((total - residues, live_ref.shape[1]), F32)
    for copy in copies[1:]:
        copy.wait()


def live_rows(live_ref, start, first, rows, pitch):
    columns = tiles(live_ref[pl.ds(first, pitch), :])
    for i in range(rows):
        yield i, (columns * row_of(live_ref, start + i)[None]).reshape(pitch, columns.shape[2])


def load_cells(cells_refs, scratch, first):
    rows, cols, channels = cells_refs[0].shape
    pitch = pad_to(cols, 16)
    for i in range(rows):
        at = (first + i) * pitch
        scratch[at : at + cols, :] = sum(ref[i].astype(F32) for ref in cells_refs)
        if pitch > cols:
            scratch[at + cols : at + pitch, :] = jnp.zeros((pitch - cols, channels), F32)


def row_of(ref, row):
    return ref[pl.ds(row, 8, stride=0), :]


def tiles(value):
    return value.reshape(value.shape[0] // 8, 8, value.shape[1])


def left_kernel(live_ref, x_ref, xp_ref, cot_ref, cotp_ref, w_ref, wg_ref,
                l_ref, lt_ref, gate_ref, cotm_ref, xs, ls, gs):
    rows, cols, channels = x_ref.shape
    pitch = pad_to(cols, 16)
    half = pad_to(rows, 16)
    hidden = w_ref.shape[1] // 4
    dap = lax.axis_index("dap")
    core = lax.rem(dap, 2)
    load_cells([x_ref], xs, 0)
    load_cells([xp_ref], xs, rows)
    normed, _ = normalize(xs[...])
    normed_half = normed.astype(BF16)
    projected = matmul(normed_half, w_ref[:, : 2 * hidden])
    left = jax.nn.sigmoid(projected[:, :hidden]) * projected[:, hidden:]
    for part, owner in enumerate((dap, dap + 1 - 2 * core)):
        for i, live in live_rows(live_ref, owner * rows, lax.axis_index("ch") * cols, rows, pitch):
            block = slice((part * rows + i) * pitch, (part * rows + i + 1) * pitch)
            value = (left[block] * live).astype(BF16).astype(F32)
            l_ref[block, :] = value
            ls[block, :] = value
    tall = pad_to(2 * rows, 16)
    ls[2 * rows * pitch :, :] = jnp.zeros(((tall - 2 * rows) * pitch, hidden), F32)
    for k in range(cols):
        lt_ref[k * tall : (k + 1) * tall, :] = ls[pl.ds(k, tall, stride=pitch), :]
    gs[...] = jax.nn.sigmoid(matmul(normed_half, wg_ref[...]))

    def pick(out_ref):
        for i in range(2 * rows):
            low = gs[i * pitch : i * pitch + rows, :]
            high = gs[i * pitch + rows : i * pitch + 2 * rows, :]
            out_ref[i * half : i * half + rows, :] = jnp.where(core == 0, low, high)
            if half > rows:
                out_ref[i * half + rows : (i + 1) * half, :] = jnp.zeros((half - rows, channels), F32)

    pick(gate_ref)
    load_cells([cot_ref], gs, 0)
    load_cells([cotp_ref], gs, rows)
    pick(cotm_ref)


def factor_kernel(live_ref, x_ref, w_ref, normed_ref, scale_ref, l1_ref, l2_ref, r1_ref, r2_ref, xs):
    rows, cols, _ = x_ref.shape
    pitch = pad_to(cols, 16)
    hidden = w_ref.shape[1] // 4
    load_cells([x_ref], xs, 0)
    normed, scale = normalize(xs[...])
    normed_ref[...] = normed
    scale_ref[...] = jnp.broadcast_to(scale, normed.shape)
    projected = matmul(normed.astype(BF16), w_ref[...])
    left_sig = jax.nn.sigmoid(projected[:, :hidden])
    right_sig = jax.nn.sigmoid(projected[:, 2 * hidden : 3 * hidden])
    left_in = projected[:, hidden : 2 * hidden] * left_sig * (1.0 - left_sig)
    right_in = projected[:, 3 * hidden :] * right_sig * (1.0 - right_sig)
    start = lax.axis_index("dap") * rows
    for i, live in live_rows(live_ref, start, lax.axis_index("ch") * cols, rows, pitch):
        block = slice(i * pitch, (i + 1) * pitch)
        l1_ref[block, :] = left_in[block] * live
        l2_ref[block, :] = left_sig[block] * live
        r1_ref[block, :] = right_in[block] * live
        r2_ref[block, :] = right_sig[block] * live


def product_part(lt_ref, rs, out, rows, cols):
    pitch, half, tall = pad_to(cols, 16), pad_to(rows, 16), pad_to(2 * rows, 16)

    def step(b, _):
        sums = [jnp.zeros((tall // 8, 8, rs.shape[1]), F32) for _ in range(JB)]
        for k in range(cols):
            left = tiles(lt_ref[k * tall : (k + 1) * tall, :])
            for n in range(JB):
                sums[n] = sums[n] + left * row_of(rs, (b * JB + n) * pitch + k)[None]
        for n in range(JB):
            out[pl.ds(b * JB + n, tall, stride=half), :] = sums[n].reshape(tall, rs.shape[1])
        return 0

    lax.fori_loop(0, rows // JB, step, 0)


def lookup(table, chip):
    value = table[0]
    for z in range(1, len(table)):
        if table[z] != table[0]:
            value = jnp.where(chip == z, table[z], value)
    return value


def turn_of(n, blocks, core):
    return n if core == 0 or n == 0 else blocks - n


def my_turn(n, blocks):
    return jnp.where(lax.axis_index("dap") % 2 == 0, turn_of(n, blocks, 0), turn_of(n, blocks, 1))


def this_chip():
    return lax.axis_index("dap") // 2


def right_of(live_ref, x_refs, w_ref, xs, rs, r_ref, s):
    rows, cols, _ = x_refs[0].shape
    pitch = pad_to(cols, 16)
    hidden = w_ref.shape[1] // 4
    load_cells(x_refs, xs, 0)
    normed, _ = normalize(xs[...])
    projected = matmul(normed.astype(BF16), w_ref[:, 2 * hidden :])
    right = jax.nn.sigmoid(projected[:, :hidden]) * projected[:, hidden:]
    start = (lax.axis_index("dap") ^ (2 * s)) * rows
    for i, live in live_rows(live_ref, start, lax.axis_index("ch") * cols, rows, pitch):
        block = slice(i * pitch, (i + 1) * pitch)
        value = (right[block] * live).astype(BF16)
        r_ref[block, :] = value
        rs[block, :] = value.astype(F32)


def part_kernel(steps, live_ref, lt_ref, w_ref, *refs):
    shards, (right_ref, part_ref, xs, rs, ps) = refs[:-5], refs[-5:]
    rows, cols, _ = shards[0].shape
    right_of(live_ref, shards, w_ref, xs, rs, right_ref, lookup(steps, this_chip()))
    product_part(lt_ref, rs, ps, rows, cols)
    part_ref[...] = ps[: part_ref.shape[0], :].astype(BF16)


def late_kernel(steps, live_ref, lt_ref, w_ref, *refs):
    blocks = len(steps)
    done, refs = refs[: blocks - 1], refs[blocks - 1 :]
    split = len(refs) - blocks - 5
    shards, right_ref, outs, (xs, rs, ps, held) = refs[:split], refs[split], refs[split + 1 : -4], refs[-4:]
    rows, cols, _ = shards[0].shape
    chip = this_chip()
    for part, table in zip(done, steps):
        held[lookup(table, chip)] = part[...]
    last = lookup(steps[-1], chip)
    right_of(live_ref, shards, w_ref, xs, rs, right_ref, last)
    product_part(lt_ref, rs, ps, rows, cols)
    held[last] = ps[: held.shape[1], :].astype(BF16)
    turn = chip ^ lax.axis_index("ch")
    for t in range(blocks):
        outs[t][...] = held[turn ^ my_turn(t, blocks)]


def middle_kernel(blocks, *refs):
    parts = refs[:blocks]
    gate_ref, cot_ref, w_ref, upd_ref, back_ref, logit_ref, gp_ref = refs[blocks:]
    total = parts[0][...].astype(F32)
    for t in range(1, blocks):
        total = total + parts[t][...].astype(F32)
    product = total.astype(BF16).astype(F32)
    hidden_norm, hidden_scale = normalize(product)
    out = matmul(hidden_norm.astype(BF16), w_ref[...])
    gate, upstream = gate_ref[...], cot_ref[...]
    grad_out = (upstream * gate).astype(BF16)
    grad_hidden = matmul_t(grad_out, w_ref[...])
    gp_ref[...] = norm_back(grad_hidden, hidden_norm, hidden_scale).astype(BF16)
    update = (gate * out).astype(BF16)
    logit = (upstream * out * gate * (1.0 - gate)).astype(BF16)
    own = upd_ref.shape[0]
    upd_ref[...] = update[:own]
    logit_ref[...] = logit[:own]
    back_ref[:own, :] = update[own:]
    back_ref[own:, :] = logit[own:]


def grad_right_part(l_ref, piece, store, rows, cols):
    pitch, half = pad_to(cols, 16), pad_to(rows, 16)

    def step(b, _):
        sums = [jnp.zeros((pitch // 8, 8, l_ref.shape[1]), F32) for _ in range(JB)]
        for i in range(2 * rows):
            left = tiles(l_ref[i * pitch : (i + 1) * pitch, :])
            for n in range(JB):
                sums[n] = sums[n] + left * row_of(piece, i * half + b * JB + n)[None]
        for n in range(JB):
            at = pl.multiple_of((b * JB + n) * pitch, pitch)
            store(pl.ds(at, pitch), sums[n].reshape(pitch, l_ref.shape[1]))
        return 0

    lax.fori_loop(0, rows // JB, step, 0)


def send_right_kernel(rows, cols, blocks, steps, *refs):
    l_ref, pieces = refs[0], refs[1 : 1 + blocks]
    more, (out_ref, gs) = refs[1 + blocks : -2], refs[-2:]
    chip, column = this_chip(), lax.axis_index("ch")
    step = lookup(steps, lax.axis_index("dap"))
    for t in range(blocks):
        @pl.when(chip ^ column ^ step == my_turn(t, blocks))
        def _(t=t):
            gs[...] = pieces[t][...].astype(F32)

    def store(where, value):
        for ref in more:
            value = value + ref[where, :].astype(F32)
        out_ref[where, :] = value.astype(BF16)

    grad_right_part(l_ref, gs, store, rows, cols)


def grad_left_part(piece_of, shard_of, first, blocks, ref, rows, cols):
    pitch, half, channels = pad_to(cols, 16), pad_to(rows, 16), ref.shape[1]

    def step(b, _):
        def block_step(m, sums):
            piece, shard = piece_of.at[m], shard_of.at[m]
            sums = list(sums)
            for j in range(rows):
                right = tiles(shard[j * pitch : (j + 1) * pitch, :])
                for n in range(JB):
                    row = (first + b * JB + n) * half + j
                    sums[n] = sums[n] + right * row_of(piece, row)[None]
            return tuple(sums)

        zero = jnp.zeros((pitch // 8, 8, channels), F32)
        sums = lax.fori_loop(0, blocks, block_step, (zero,) * JB)
        for n in range(JB):
            at = pl.multiple_of((b * JB + n) * pitch, pitch)
            ref[pl.ds(at, pitch), :] = sums[n].reshape(pitch, channels).astype(ref.dtype)
        return 0

    lax.fori_loop(0, rows // JB, step, 0)


def pair_left_kernel(rows, cols, steps, *refs):
    blocks = len(steps)
    pieces, shards, (send_ref, gs, rs) = refs[:blocks], refs[blocks : 2 * blocks], refs[2 * blocks :]
    chip, column = this_chip(), lax.axis_index("ch")
    for t in range(blocks):
        gs[column ^ my_turn(t, blocks)] = pieces[t][...].astype(F32)
    for table, shard in zip(steps, shards):
        rs[chip ^ lookup(table, chip)] = shard[...].astype(F32)
    grad_left_part(gs, rs, rows, blocks, send_ref, rows, cols)


def own_kernel(rows, cols, blocks, l_ref, gs, rs, left_ref, right_ref):
    grad_left_part(gs, rs, 0, blocks, left_ref, rows, cols)

    def store(where, value):
        right_ref[where, :] = value

    grad_right_part(l_ref, gs.at[this_chip()], store, rows, cols)


def finish_left_kernel(own_ref, got_ref, l1_ref, l2_ref, w_ref, wg_ref, upd_ref, logit_ref, back_ref,
                       out_ref, acc_ref, us, gs):
    rows, cols, channels = out_ref.shape
    pitch, half = pad_to(cols, 16), pad_to(rows, 16)
    mine = lax.rem(lax.axis_index("dap"), 2) == 0
    for i in range(rows):
        for scratch, ref, base in ((us, upd_ref, 0), (gs, logit_ref, rows * half)):
            here = ref[i * half : (i + 1) * half, :].astype(F32)[:rows]
            there = back_ref[base + i * half : base + (i + 1) * half, :].astype(F32)[:rows]
            scratch[i * pitch : i * pitch + rows, :] = jnp.where(mine, here, there)
            scratch[i * pitch + rows : i * pitch + 2 * rows, :] = jnp.where(mine, there, here)
            if pitch > cols:
                scratch[i * pitch + cols : (i + 1) * pitch, :] = jnp.zeros((pitch - cols, channels), F32)
        out_ref[i] = us[i * pitch : i * pitch + cols, :].astype(BF16)
    grad_left = (own_ref[...] + got_ref[...].astype(F32)).astype(BF16).astype(F32)
    hidden = own_ref.shape[1]
    acc = matmul_t((grad_left * l1_ref[...]).astype(BF16), w_ref[:, :hidden])
    acc = acc + matmul_t((grad_left * l2_ref[...]).astype(BF16), w_ref[:, hidden : 2 * hidden])
    acc_ref[...] = acc + matmul_t(gs[...].astype(BF16), wg_ref[...])


def finish_kernel(count, *refs):
    parts = refs[:count]
    r1_ref, r2_ref, w_ref, acc_ref, normed_ref, scale_ref, out_ref = refs[count:]
    rows, cols, _ = out_ref.shape
    pitch = pad_to(cols, 16)
    total = parts[0][...]
    for s in range(1, count):
        total = total + parts[s][...].astype(F32)
    grad_right = total.astype(BF16).astype(F32)
    hidden = total.shape[1]
    grad = acc_ref[...] + matmul_t((grad_right * r1_ref[...]).astype(BF16), w_ref[:, 2 * hidden : 3 * hidden])
    grad = grad + matmul_t((grad_right * r2_ref[...]).astype(BF16), w_ref[:, 3 * hidden :])
    result = norm_back(grad, normed_ref[...], scale_ref[...]).astype(BF16)
    for i in range(rows):
        out_ref[i] = result[i * pitch : i * pitch + cols]


VMEM = pl.BlockSpec(memory_space=pltpu.VMEM)
HBM = pl.BlockSpec(memory_space=pltpu.HBM)


def call(body, outs, args, scratch=(), specs=VMEM, flops=10**7):
    outs = [jax.ShapeDtypeStruct(shape, dtype) for shape, dtype in outs]
    moved = sum(a.size * a.dtype.itemsize for a in [*args, *outs])
    scratch = [pltpu.VMEM(shape, F32) if isinstance(shape, tuple) else shape for shape in scratch]
    return pl.pallas_call(
        body,
        out_shape=outs,
        in_specs=[specs] * len(args),
        out_specs=[VMEM] * len(outs),
        scratch_shapes=scratch,
        compiler_params=pltpu.CompilerParams(vmem_limit_bytes=20 << 20),
        cost_estimate=pl.CostEstimate(flops=flops, bytes_accessed=moved, transcendentals=0),
    )(*args)


def on_device(devices, blocks, x, mask, w_proj, w_gate, w_out, cot):
    rows, cols, channels = x.shape
    hidden = w_out.shape[0]
    pitch, half, tall = pad_to(cols, 16), pad_to(rows, 16), pad_to(2 * rows, 16)
    cells, wide, mids = rows * pitch, 2 * rows * pitch, 2 * rows * half
    if devices != 2 * blocks or cols != 2 * rows or blocks & (blocks - 1) or rows % JB:
        raise ValueError("unsupported split")

    def along_dap(value, pairs):
        return lax.ppermute(value, "dap", [(2 * a + c, 2 * b + c) for a, b in pairs for c in range(2)])

    def along_ch(value, t):
        return lax.ppermute(value, ("dap", "ch"), [
            (d * blocks + h, d * blocks + (h ^ turn_of(t, blocks, d % 2))) for d in range(devices) for h in range(blocks)])

    def to_partner(value):
        return lax.ppermute(value, "dap", [(d, d ^ 1) for d in range(devices)])

    moves, shards = gather_plan(blocks)
    moved = []
    for pairs, source in moves:
        moved.append(along_dap(x if source is None else moved[source], pairs))
    x_pair, cot_pair = to_partner(x), to_partner(cot)
    sources = (x, cot, w_proj, w_gate, w_out)
    residues = mask.shape[0]
    xv, cotv, w_proj, w_gate, w_out, live = call(
        load_kernel,
        [(a.shape, a.dtype) for a in sources] + [((pad_to(residues + pitch - cols, 8), channels), F32)],
        [pltpu.with_memory_space_constraint(a, pltpu.HBM) for a in (mask, *sources)], [pltpu.SemaphoreType.DMA((6,)), pltpu.SMEM((residues,), jnp.int32)], specs=HBM)
    left, left_t, gate, upstream = call(
        left_kernel,
        [((wide, hidden), F32), ((cols * tall, hidden), F32), ((mids, channels), F32), ((mids, channels), F32)],
        (live, xv, x_pair, cotv, cot_pair, w_proj, w_gate),
        [(wide, channels), (tall * pitch, hidden), (wide, channels)])
    scratch = [(cells, channels), (cells, hidden), (tall * half, hidden)]
    steps = [[0] * blocks] + [table for _, table in shards]
    held = [[xv]] + [[moved[n] for n in group] for group, _ in shards]
    rights, done = [], []
    for s in range(blocks - 1):
        right, part = call(
            functools.partial(part_kernel, steps[s]), [((cells, hidden), BF16), ((mids, hidden), BF16)],
            (live, left_t, w_proj, *held[s]), scratch)
        rights.append(right)
        done.append(part)
    right, *parts = call(
        functools.partial(late_kernel, steps), [((cells, hidden), BF16)] + [((mids, hidden), BF16)] * blocks,
        (live, left_t, w_proj, *done, *held[-1]), scratch + [pltpu.VMEM((blocks, mids, hidden), BF16)])
    rights.append(right)
    for t in range(1, blocks):
        parts[t] = along_ch(parts[t], t)
    update, back, logit, grad_product = call(
        functools.partial(middle_kernel, blocks),
        [((mids // 2, channels), BF16), ((mids, channels), BF16), ((mids // 2, channels), BF16), ((mids, hidden), BF16)],
        (*parts, gate, upstream, w_out))
    pieces = [grad_product] + [along_ch(grad_product, t) for t in range(1, blocks)]
    back = to_partner(back)
    sends, returns, arrivals = reduce_plan(blocks)
    got = []
    for n, (table, extra) in enumerate(sends):
        more = () if extra is None else (got[extra],)
        (send,) = call(functools.partial(send_right_kernel, rows, cols, blocks, table),
                       [((cells, hidden), BF16)], (left, *pieces, *more), [(mids, hidden)])
        got.append(lax.ppermute(send, "dap", returns[n][0]))
    left_send, staged, rights_staged = call(
        functools.partial(pair_left_kernel, rows, cols, steps),
        [((cells, hidden), BF16), ((blocks, mids, hidden), F32), ((blocks, cells, hidden), F32)], (*pieces, *rights))
    left_got = to_partner(left_send)
    left_own, right_own = call(
        functools.partial(own_kernel, rows, cols, blocks), [((cells, hidden), F32)] * 2,
        (left, staged, rights_staged))
    normed, scale, l1, l2, r1, r2 = call(
        factor_kernel, [((cells, hidden), F32)] * 6, (live, xv, w_proj),
        [(cells, channels)])
    pair_update, acc = call(
        finish_left_kernel, [((rows, cols, channels), BF16), ((cells, channels), F32)],
        (left_own, left_got, l1, l2, w_proj, w_gate, update, logit, back),
        [(cells, channels), (cells, channels)])
    (grad_pair,) = call(functools.partial(finish_kernel, 1 + len(arrivals)), [((rows, cols, channels), BF16)],
                        (right_own, *[got[n] for n in arrivals], r1, r2, w_proj, acc, normed, scale))
    return pair_update, grad_pair


def gather_plan(blocks):
    order = [*range(2, blocks, 2), 1, *range(3, blocks, 2)]
    moves = []
    for s in order:
        relay = s % 2 and s > 1
        moves.append(([(z, z ^ (1 if relay else s)) for z in range(blocks)], order.index(s ^ 1) if relay else None))
    return moves, [([n], [s] * blocks) for n, s in enumerate(order)]


def reduce_plan(blocks):
    far = [*range(2, blocks), 1]
    odd = [*range(blocks - 1, 0, -1)]
    sends = [([a, b] * blocks, None) for a, b in zip(far, odd)]
    return sends, [[[(2 * z + c, 2 * (z ^ s) + c) for z in range(blocks) for c, s in enumerate(pair)]] for pair in zip(far, odd)], [*range(blocks - 1)]


def solution(mesh):
    blocks = mesh.shape["ch"]

    def body(*args):
        return on_device(mesh.shape["dap"], blocks, *args)

    return jax.shard_map(
        body,
        mesh=mesh,
        in_specs=(P("dap", "ch", None), P(), P(), P(), P(), P("dap", "ch", None)),
        out_specs=(P("dap", "ch", None), P("dap", "ch", None)),
        check_vma=False,
    )
```
